512 devices in a mesh: tm: 8 (over x, core), azim: 64 (over z, y).
Axes of the slice: x: 4, y: 8, z: 8, core: 2. Of those that a mesh axis runs over, the one named last changes fastest.
Arguments:
- pressure: bfloat16 [256, 160, 1024], P('azim', None, 'tm'), may hold values from -6 to 6
Outputs:
- gram_xx: float32 [128, 2, 1024, 1024], P('azim', None, 'tm')
- gram_xy: float32 [128, 2, 1024, 1024], P('azim', None, 'tm')
The draws below stay inside these ranges and needn't reach their ends.
All inputs are finite; a program needn't handle non-finite values.
Results may differ from the reference program's by a relative error of at most 0.0046.
Values may be sent and summed in bfloat16 or wider, within the bound.
No kernel may reach another device: no remote copies, remote signals or barrier semaphores. Data moves between devices by JAX's collectives and lax.ppermute only.
A program may use at most 64 MiB of HBM per device.

```python
import jax
import jax.numpy as jnp
from jax import lax

THETA = 256
MODES = 128
ROWS = 160
SNAP_DEV = 128
SNAP = 1024


def shard_levels(stream_key, extent, cuts, smallest, top_value):
    def one(axis_at, parts):
        heights = jax.random.uniform(jax.random.fold_in(jax.random.fold_in(stream_key, 6), axis_at), (parts,), jnp.float32, smallest / len(cuts), top_value / len(cuts))
        return jnp.repeat(jnp.exp(heights), extent[axis_at] // parts).reshape((-1,) + (1,) * (len(extent) - axis_at - 1))

    loudness = one(*cuts[0])
    for cut in cuts[1:]:
        loudness = loudness * one(*cut)
    return loudness


def normal_values(own_key, extent, width, reach, cuts=(), kind=jnp.bfloat16):
    values = jax.random.normal(own_key, extent, jnp.float32) * width
    if len(cuts) > 0:
        values = shard_levels(own_key, extent, cuts, -0.22, 0.18) * values
    return jnp.clip(values, min=-reach, max=reach).astype(kind)


def setup_inputs(seed: int = 0) -> dict:
    key_list = jax.random.split(jax.random.key(seed), 2)
    pressure = normal_values(key_list[0], (THETA, ROWS, SNAP), 1.0, 6.0, ((0, 64), (2, 8)))
    return dict(pressure=pressure)


def tables():
    angle_idx = jnp.arange(THETA, dtype=jnp.int32)[:, None]
    wave_idx = jnp.arange(MODES, dtype=jnp.int32)[None, :]
    phase = ((angle_idx * wave_idx) % THETA).astype(jnp.float32) * (2.0 * jnp.pi / THETA)
    scale = THETA ** -0.5
    return (jnp.cos(phase) * scale).astype(jnp.bfloat16), (-jnp.sin(phase) * scale).astype(jnp.bfloat16)


def reference(pressure):
    table_cos, table_sin = tables()
    field = pressure.astype(jnp.float32)
    real_part = jnp.einsum("art,am->mrt", field, table_cos.astype(jnp.float32)).astype(jnp.bfloat16)
    imag_part = jnp.einsum("art,am->mrt", field, table_sin.astype(jnp.float32)).astype(jnp.bfloat16)
    modes = jnp.stack([real_part, imag_part], axis=1)
    shifted = jnp.concatenate([modes[..., 1:], jnp.zeros(modes.shape[:3] + (1,), jnp.bfloat16)], axis=3)
    gain = ROWS ** -0.5
    rows_blk = jnp.arange(SNAP, dtype=jnp.int32)[:, None] // SNAP_DEV
    cols_blk = jnp.arange(SNAP, dtype=jnp.int32)[None, :] // SNAP_DEV
    keep = cols_blk <= rows_blk

    def gram(left, right):
        left = left.astype(jnp.float32)
        right = right.astype(jnp.float32)
        real = jnp.dot(left[0].T, right[0], preferred_element_type=jnp.float32) + jnp.dot(left[1].T, right[1], preferred_element_type=jnp.float32)
        imag = jnp.dot(left[0].T, right[1], preferred_element_type=jnp.float32) - jnp.dot(left[1].T, right[0], preferred_element_type=jnp.float32)
        both = jnp.stack([real, imag]) * gain
        return jnp.where(keep[None], both, jnp.float32(0.0))

    def per_mode(items):
        left, right = items
        return gram(left, left), gram(left, right)

    gram_xx, gram_xy = lax.map(per_mode, (modes, shifted))
    return gram_xx, gram_xy
```

```python
import jax
import jax.numpy as jnp
import numpy as np
from jax import lax
from jax.experimental import pallas as pl
from jax.experimental.pallas import tpu as pltpu
from jax.sharding import PartitionSpec as P

THETA = 256
MODES = 128
ROWS = 160
LANES = 128
HALF = 64
PARTS = 64
FIVE = 5
CELL = 2 * FIVE


def make_table():
    b, alo, p, k, ahi, s = np.meshgrid(
        np.arange(2), np.arange(2), np.arange(2), np.arange(64), np.arange(2), np.arange(64), indexing="ij"
    )
    angle = 4 * s + 2 * ahi + alo
    wave = 2 * k + b
    phase = ((angle * wave) % THETA).astype(np.float32) * np.float32(2.0 * np.pi / THETA)
    values = np.where(p == 1, -np.sin(phase), np.cos(phase)) * np.float32(THETA ** (-0.5))
    return values.astype(np.float32).reshape(512, 128).astype(jnp.bfloat16)


def low_lanes(shape):
    return lax.broadcasted_iota(jnp.int32, shape, 1) < HALF


def spread_kernel(x_ref, o_ref, scr):
    low = low_lanes((ROWS, LANES))
    for ahi in range(2):
        even = x_ref[2 * ahi].astype(jnp.float32)
        odd = x_ref[2 * ahi + 1].astype(jnp.float32)
        scr[pl.ds(ahi, ROWS, stride=2), :] = jnp.where(low, even, pltpu.roll(odd, HALF, 1))
        scr[pl.ds(2 * ROWS + ahi, ROWS, stride=2), :] = jnp.where(low, pltpu.roll(even, HALF, 1), odd)
    o_ref[...] = scr[...].astype(jnp.bfloat16)


def transform_kernel(x_ref, t_ref, o_ref, scr_in, scr_out):
    scr_in[...] = x_ref[...].astype(jnp.float32)
    low = low_lanes((LANES, LANES))
    for r5 in range(FIVE):
        field = jnp.concatenate(
            [scr_in[pl.ds(2 * r5 + ahi, PARTS, stride=CELL), :] for ahi in range(2)], axis=0
        ).astype(jnp.bfloat16)
        y = jnp.dot(t_ref[...], field, preferred_element_type=jnp.float32)
        straight = jnp.where(low, y[0:128], y[384:512])
        crossed = jnp.where(low, y[256:384], y[128:256])
        both = straight + pltpu.roll(crossed, HALF, 1)
        for p in range(2):
            scr_out[pl.ds(2 * r5 + p, PARTS, stride=CELL), :] = both[64 * p : 64 * p + 64]
    o_ref[...] = scr_out[...].astype(jnp.bfloat16)


def gram_kernel(idx_ref, a_ref, b_ref, xx_ref, xy_ref, right, left):
    step = pl.program_id(0)
    tm = idx_ref[0]
    core = lax.rem(tm, 2)

    @pl.when(step == 0)
    def _():
        low = low_lanes((2 * ROWS, LANES))
        for own, ref in ((True, a_ref), (False, b_ref)):
            par = core if own else 1 - core
            for x in range(4):
                first = ref[x, 0 : 2 * ROWS].astype(jnp.float32)
                second = ref[x, 2 * ROWS : 4 * ROWS].astype(jnp.float32)
                at = pl.multiple_of((2 * x + par) * LANES, LANES)
                right[0, :, pl.ds(at, LANES)] = jnp.where(low, first, pltpu.roll(second, HALF, 1)).astype(jnp.bfloat16)
                right[1, :, pl.ds(at, LANES)] = jnp.where(low, pltpu.roll(first, HALF, 1), second).astype(jnp.bfloat16)
        even = lax.rem(lax.broadcasted_iota(jnp.int32, (2 * ROWS, LANES), 0), 2) == 0
        here = pl.multiple_of(tm * LANES, LANES)
        for m in range(2):
            f = right[m, :, pl.ds(here, LANES)].astype(jnp.float32)
            turned = jnp.where(even, -pltpu.roll(f, 2 * ROWS - 1, 0), pltpu.roll(f, 1, 0))
            left[2 * m] = f.T.astype(jnp.bfloat16)
            left[2 * m + 1] = turned.T.astype(jnp.bfloat16)

    g = jnp.dot(left[step], right[step // 2], preferred_element_type=jnp.float32) * jnp.float32(ROWS ** (-0.5))
    col = lax.broadcasted_iota(jnp.int32, g.shape, 1)
    keep = col < (tm + 1) * LANES
    xx_ref[0, 0] = jnp.where(keep, g, 0.0)
    xy_ref[0, 0] = jnp.where(keep & (col < g.shape[1] - 1), pltpu.roll(g, g.shape[1] - 1, 1), 0.0)


def body(pressure):
    f32 = jnp.float32
    bf16 = jnp.bfloat16
    tm = lax.axis_index("tm")
    send = pl.pallas_call(
        spread_kernel,
        out_shape=jax.ShapeDtypeStruct((640, LANES), bf16),
        scratch_shapes=[pltpu.VMEM((640, LANES), f32)],
        name="spread",
    )(pressure)
    got = lax.all_to_all(send.reshape(PARTS, FIVE, 2, LANES), "azim", 0, 0, tiled=True)
    spectrum = pl.pallas_call(
        transform_kernel,
        out_shape=jax.ShapeDtypeStruct((640, LANES), bf16),
        scratch_shapes=[pltpu.VMEM((640, LANES), f32), pltpu.VMEM((640, LANES), f32)],
        name="transform",
    )(got.reshape(640, LANES), jnp.asarray(make_table()))
    owned = lax.all_to_all(spectrum.reshape(PARTS, FIVE, 2, LANES), "azim", 0, 0, tiled=True)
    owned = owned.reshape(640, LANES)
    chips = [[2 * x + c for x in range(4)] for c in range(2)]
    mine = lax.all_to_all(
        jnp.broadcast_to(owned[None], (4, 640, LANES)), "tm", 0, 0, tiled=True, axis_index_groups=chips
    )
    theirs = lax.ppermute(mine, "tm", [(i, i ^ 1) for i in range(8)])
    out = jax.ShapeDtypeStruct((2, 2, LANES, 1024), f32)
    block = pl.BlockSpec((1, 1, LANES, 1024), lambda i, idx: (i // 2, i % 2, 0, 0))
    whole = pl.BlockSpec((4, 640, LANES), lambda i, idx: (0, 0, 0))
    return pl.pallas_call(
        gram_kernel,
        grid_spec=pltpu.PrefetchScalarGridSpec(
            num_scalar_prefetch=1,
            grid=(4,),
            in_specs=[whole, whole],
            out_specs=[block, block],
            scratch_shapes=[pltpu.VMEM((2, 2 * ROWS, 1024), bf16), pltpu.VMEM((4, LANES, 2 * ROWS), bf16)],
        ),
        out_shape=(out, out),
        name="gram",
    )(tm.astype(jnp.int32).reshape(1), mine, theirs)


def solution(mesh):
    in_specs = (P("azim", None, "tm"),)
    out_specs = (P("azim", None, "tm", None), P("azim", None, "tm", None))
    return jax.shard_map(body, mesh=mesh, in_specs=in_specs, out_specs=out_specs, check_vma=False)
```

```python
import jax
import jax.numpy as jnp
import numpy as np
from jax import lax
from jax.experimental import pallas as pl
from jax.experimental.pallas import tpu as pltpu
from jax.sharding import PartitionSpec as P

THETA = 256
MODES = 128
ROWS = 160
LANES = 128
HALF = 64
PARTS = 64
FIVE = 5
CELL = 2 * FIVE


def make_table():
    b, alo, p, k, ahi, s = np.meshgrid(
        np.arange(2), np.arange(2), np.arange(2), np.arange(64), np.arange(2), np.arange(64), indexing="ij"
    )
    angle = 4 * s + 2 * ahi + alo
    wave = 2 * k + b
    phase = ((angle * wave) % THETA).astype(np.float32) * np.float32(2.0 * np.pi / THETA)
    values = np.where(p == 1, -np.sin(phase), np.cos(phase)) * np.float32(THETA ** (-0.5))
    return values.astype(np.float32).reshape(512, 128).astype(jnp.bfloat16)


def low_lanes(shape):
    return lax.broadcasted_iota(jnp.int32, shape, 1) < HALF


def spread_kernel(x_ref, o_ref, scr):
    low = low_lanes((ROWS, LANES))
    for ahi in range(2):
        even = x_ref[2 * ahi].astype(jnp.float32)
        odd = x_ref[2 * ahi + 1].astype(jnp.float32)
        scr[pl.ds(ahi, ROWS, stride=2), :] = jnp.where(low, even, pltpu.roll(odd, HALF, 1))
        scr[pl.ds(2 * ROWS + ahi, ROWS, stride=2), :] = jnp.where(low, pltpu.roll(even, HALF, 1), odd)
    o_ref[...] = scr[...].astype(jnp.bfloat16)


def transform_kernel(x_ref, t_ref, o_ref, scr_in, scr_out):
    half = lax.axis_index("azim") // (PARTS // 2)
    one = t_ref[pl.ds(pl.multiple_of(256 * half, 256), 256)]
    two = t_ref[pl.ds(pl.multiple_of(256 * (1 - half), 256), 256)]
    scr_in[...] = x_ref[...].astype(jnp.float32)
    low = low_lanes((LANES, LANES))
    for r5 in range(FIVE):
        field = jnp.concatenate(
            [scr_in[pl.ds(2 * r5 + ahi, PARTS, stride=CELL), :] for ahi in range(2)], axis=0
        ).astype(jnp.bfloat16)
        y = jnp.dot(one, field, preferred_element_type=jnp.float32)
        w = jnp.dot(two, field, preferred_element_type=jnp.float32)
        straight = jnp.where(low, y[0:128], w[128:256])
        crossed = jnp.where(low, w[0:128], y[128:256])
        both = straight + pltpu.roll(crossed, HALF, 1)
        for p in range(2):
            scr_out[pl.ds(2 * r5 + p, PARTS, stride=CELL), :] = both[64 * p : 64 * p + 64]
    o_ref[...] = scr_out[...].astype(jnp.bfloat16)


def gram_kernel(idx_ref, a_ref, b_ref, xx_ref, xy_ref, right, left):
    m = pl.program_id(0)
    tm = idx_ref[0]
    core = lax.rem(tm, 2)

    @pl.when(m == 0)
    def _():
        low = low_lanes((2 * ROWS, LANES))
        for own, ref in ((True, a_ref), (False, b_ref)):
            par = core if own else 1 - core
            for x in range(4):
                first = ref[x, 0 : 2 * ROWS]
                second = ref[x, 2 * ROWS : 4 * ROWS]
                at = pl.multiple_of((2 * x + par) * LANES, LANES)
                right[0, :, pl.ds(at, LANES)] = jnp.where(low, first, second)
                right[1, :, pl.ds(at, LANES)] = pltpu.roll(jnp.where(low, second, first), HALF, 1)
        even = lax.rem(lax.broadcasted_iota(jnp.int32, (2 * ROWS, LANES), 0), 2) == 0
        here = pl.multiple_of(tm * LANES, LANES)
        for n in range(2):
            f = right[n, :, pl.ds(here, LANES)].astype(jnp.float32)
            turned = jnp.where(even, -pltpu.roll(f, 2 * ROWS - 1, 0), pltpu.roll(f, 1, 0))
            left[n, :LANES] = f.T.astype(jnp.bfloat16)
            left[n, LANES:] = turned.T.astype(jnp.bfloat16)

    g = jnp.dot(left[m], right[m], preferred_element_type=jnp.float32) * jnp.float32(ROWS ** (-0.5))
    col = lax.broadcasted_iota(jnp.int32, g.shape, 1)
    keep = col < (tm + 1) * LANES
    xx = jnp.where(keep, g, 0.0)
    xy = jnp.where(keep & (col < g.shape[1] - 1), pltpu.roll(g, g.shape[1] - 1, 1), 0.0)
    for p in range(2):
        xx_ref[0, p] = xx[p * LANES : (p + 1) * LANES]
        xy_ref[0, p] = xy[p * LANES : (p + 1) * LANES]


def near(array):
    return pltpu.with_memory_space_constraint(array, pltpu.VMEM)


def body(pressure):
    f32 = jnp.float32
    bf16 = jnp.bfloat16
    tm = lax.axis_index("tm")
    vmem = pl.BlockSpec(memory_space=pltpu.VMEM)
    send = pl.pallas_call(
        spread_kernel,
        out_shape=pltpu.VMEM((640, LANES), bf16),
        in_specs=[vmem],
        out_specs=vmem,
        scratch_shapes=[pltpu.VMEM((640, LANES), f32)],
        name="spread",
    )(pressure)
    got = lax.all_to_all(send.reshape(PARTS, FIVE, 2, LANES), "azim", 0, 0, tiled=True)
    spectrum = pl.pallas_call(
        transform_kernel,
        out_shape=pltpu.VMEM((640, LANES), bf16),
        in_specs=[vmem, vmem],
        out_specs=vmem,
        scratch_shapes=[pltpu.VMEM((640, LANES), f32), pltpu.VMEM((640, LANES), f32)],
        name="transform",
    )(near(got.reshape(640, LANES)), near(jnp.asarray(make_table())))
    owned = lax.all_to_all(spectrum.reshape(PARTS, FIVE, 2, LANES), "azim", 0, 0, tiled=True)
    owned = owned.reshape(640, LANES)
    chips = [[2 * x + c for x in range(4)] for c in range(2)]
    mine = lax.all_to_all(
        jnp.broadcast_to(owned[None], (4, 640, LANES)), "tm", 0, 0, tiled=True, axis_index_groups=chips
    )
    theirs = lax.ppermute(mine, "tm", [(i, i ^ 1) for i in range(8)])
    out = jax.ShapeDtypeStruct((2, 2, LANES, 1024), f32)
    block = pl.BlockSpec((1, 2, LANES, 1024), lambda i, idx: (i, 0, 0, 0))
    return pl.pallas_call(
        gram_kernel,
        grid_spec=pltpu.PrefetchScalarGridSpec(
            num_scalar_prefetch=1,
            grid=(2,),
            in_specs=[vmem, vmem],
            out_specs=[block, block],
            scratch_shapes=[pltpu.VMEM((2, 2 * ROWS, 1024), bf16), pltpu.VMEM((2, 2 * LANES, 2 * ROWS), bf16)],
        ),
        out_shape=(out, out),
        name="gram",
    )(tm.astype(jnp.int32).reshape(1), near(mine), near(theirs))


def solution(mesh):
    in_specs = (P("azim", None, "tm"),)
    out_specs = (P("azim", None, "tm", None), P("azim", None, "tm", None))
    return jax.shard_map(body, mesh=mesh, in_specs=in_specs, out_specs=out_specs, check_vma=False)
```

```python
import jax
import jax.numpy as jnp
import numpy as np
from jax import lax
from jax.experimental import pallas as pl
from jax.experimental.pallas import tpu as pltpu
from jax.sharding import PartitionSpec as P

THETA = 256
MODES = 128
ROWS = 160
LANES = 128
HALF = 64
PARTS = 64
FIVE = 5
CELL = 2 * FIVE


def make_table():
    b, alo, p, k, ahi, s = np.meshgrid(
        np.arange(2), np.arange(2), np.arange(2), np.arange(64), np.arange(2), np.arange(64), indexing="ij"
    )
    angle = 4 * s + 2 * ahi + alo
    wave = 2 * k + b
    phase = ((angle * wave) % THETA).astype(np.float32) * np.float32(2.0 * np.pi / THETA)
    values = np.where(p == 1, -np.sin(phase), np.cos(phase)) * np.float32(THETA ** (-0.5))
    return values.astype(np.float32).reshape(512, 128).astype(jnp.bfloat16)


def low_lanes(shape):
    return lax.broadcasted_iota(jnp.int32, shape, 1) < HALF


def spread_kernel(x_ref, t_ref, o_ref, table_ref, near_ref, scr, sems):
    fetch = [
        pltpu.make_async_copy(x_ref.at[pl.ds(2 * ahi, 2)], near_ref.at[pl.ds(2 * ahi, 2)], sems.at[ahi])
        for ahi in range(2)
    ]
    fetch.append(pltpu.make_async_copy(t_ref, table_ref, sems.at[2]))
    for copy in fetch:
        copy.start()
    low = low_lanes((ROWS, LANES))
    for ahi in range(2):
        fetch[ahi].wait()
        even = near_ref[2 * ahi].astype(jnp.float32)
        odd = near_ref[2 * ahi + 1].astype(jnp.float32)
        scr[pl.ds(ahi, ROWS, stride=2), :] = jnp.where(low, even, pltpu.roll(odd, HALF, 1))
        scr[pl.ds(2 * ROWS + ahi, ROWS, stride=2), :] = jnp.where(low, pltpu.roll(even, HALF, 1), odd)
    o_ref[...] = scr[...].astype(jnp.bfloat16)
    fetch[2].wait()


def transform_kernel(x_ref, t_ref, o_ref, scr_in, scr_out):
    half = lax.axis_index("azim") // (PARTS // 2)
    one = t_ref[pl.ds(pl.multiple_of(256 * half, 256), 256)]
    two = t_ref[pl.ds(pl.multiple_of(256 * (1 - half), 256), 256)]
    scr_in[...] = x_ref[...].astype(jnp.float32)
    low = low_lanes((LANES, LANES))
    for r5 in range(FIVE):
        field = jnp.concatenate(
            [scr_in[pl.ds(2 * r5 + ahi, PARTS, stride=CELL), :] for ahi in range(2)], axis=0
        ).astype(jnp.bfloat16)
        y = jnp.dot(one, field, preferred_element_type=jnp.float32)
        w = jnp.dot(two, field, preferred_element_type=jnp.float32)
        straight = jnp.where(low, y[0:128], w[128:256])
        crossed = jnp.where(low, w[0:128], y[128:256])
        both = straight + pltpu.roll(crossed, HALF, 1)
        for p in range(2):
            scr_out[pl.ds(2 * r5 + p, PARTS, stride=CELL), :] = both[64 * p : 64 * p + 64]
    o_ref[...] = scr_out[...].astype(jnp.bfloat16)


GAIN = ROWS ** (-0.5)
CHIPS = 4
WIDE = CHIPS * LANES
GRANT = pltpu.CompilerParams(vmem_limit_bytes=16 << 20)


def mode_rows(ref, x, m):
    low = low_lanes((2 * ROWS, LANES))
    first = ref[x, 0 : 2 * ROWS]
    second = ref[x, 2 * ROWS : 4 * ROWS]
    if m == 0:
        return jnp.where(low, first, second)
    return pltpu.roll(jnp.where(low, second, first), HALF, 1)


def wide_rows(ref, m):
    return jnp.concatenate([mode_rows(ref, x, m) for x in range(CHIPS)], axis=1)


def tile_copy(src, dst, m, x, par, sem):
    at = pl.multiple_of((2 * x + par) * LANES, LANES)
    return pltpu.make_async_copy(src.at[m, x], dst.at[m, :, :, pl.ds(at, LANES)], sem)


def store_tile(ref, m, x, value):
    ref[m, x, 0] = value[:LANES]
    ref[m, x, 1] = value[LANES:]


def own_kernel(mine_ref, xx_ref, left_ref, next_ref, tile, sems):
    tm = lax.axis_index("tm")
    core = lax.rem(tm, 2)
    even = lax.rem(lax.broadcasted_iota(jnp.int32, (2 * ROWS, LANES), 0), 2) == 0
    for m in range(2):
        f = mode_rows(mine_ref, lax.div(tm, 2), m).astype(jnp.float32)
        turned = jnp.where(even, -pltpu.roll(f, 2 * ROWS - 1, 0), pltpu.roll(f, 1, 0))
        left_ref[m, :LANES] = f.T.astype(jnp.bfloat16)
        left_ref[m, LANES:] = turned.T.astype(jnp.bfloat16)
        g = jnp.dot(left_ref[m], wide_rows(mine_ref, m), preferred_element_type=jnp.float32) * jnp.float32(GAIN)
        for x in range(CHIPS):
            block = g[:, x * LANES : (x + 1) * LANES]
            store_tile(tile, m, x, jnp.where(2 * x + core <= tm, block, 0.0))
            tile_copy(tile, xx_ref, m, x, core, sems.at[m, x]).start()
            next_ref[m, x] = pltpu.roll(block, LANES - 1, 1)
        next_ref[m, CHIPS] = jnp.zeros((2 * LANES, LANES), jnp.float32)
    for m in range(2):
        for x in range(CHIPS):
            tile_copy(tile, xx_ref, m, x, core, sems.at[m, x]).wait()


def partner_kernel(theirs_ref, left_ref, next_ref, old_ref, xx_ref, xy_ref, tile, pair, ynext, sems, ysems):
    del old_ref
    tm = lax.axis_index("tm")
    core = lax.rem(tm, 2)
    other = 1 - core
    inner = lax.broadcasted_iota(jnp.int32, (2 * LANES, LANES), 1) < LANES - 1
    for m in range(2):
        g = jnp.dot(left_ref[m], wide_rows(theirs_ref, m), preferred_element_type=jnp.float32) * jnp.float32(GAIN)
        for x in range(CHIPS):
            block = g[:, x * LANES : (x + 1) * LANES]
            keep = 2 * x + other <= tm
            store_tile(tile, m, x, jnp.where(keep, block, 0.0))
            tile_copy(tile, xx_ref, m, x, other, sems.at[m, x]).start()
            shifted = pltpu.roll(block, LANES - 1, 1)
            ynext[m, x] = shifted
            whole = jnp.where(inner, shifted, next_ref[m, x + 1 - core])
            store_tile(pair.at[1], m, x, jnp.where(keep, whole, 0.0))
            tile_copy(pair.at[1], xy_ref, m, x, other, ysems.at[1, m, x]).start()
        ynext[m, CHIPS] = jnp.zeros((2 * LANES, LANES), jnp.float32)
        for x in range(CHIPS):
            whole = jnp.where(inner, next_ref[m, x], ynext[m, x + core])
            store_tile(pair.at[0], m, x, jnp.where(2 * x + core <= tm, whole, 0.0))
            tile_copy(pair.at[0], xy_ref, m, x, core, ysems.at[0, m, x]).start()
    for m in range(2):
        for x in range(CHIPS):
            tile_copy(tile, xx_ref, m, x, other, sems.at[m, x]).wait()
            tile_copy(pair.at[1], xy_ref, m, x, other, ysems.at[1, m, x]).wait()
            tile_copy(pair.at[0], xy_ref, m, x, core, ysems.at[0, m, x]).wait()


def near(array):
    return pltpu.with_memory_space_constraint(array, pltpu.VMEM)


def kept(array):
    return pltpu.with_memory_space_constraint(array, pltpu.HBM)


def body(pressure):
    f32 = jnp.float32
    bf16 = jnp.bfloat16
    vmem = pl.BlockSpec(memory_space=pltpu.VMEM)
    hbm = pl.BlockSpec(memory_space=pl.ANY)
    far = pl.BlockSpec(memory_space=pltpu.HBM)
    table = jnp.asarray(make_table())
    send, table = pl.pallas_call(
        spread_kernel,
        out_shape=(pltpu.VMEM((640, LANES), bf16), pltpu.VMEM(table.shape, bf16)),
        in_specs=[far, far],
        out_specs=(vmem, vmem),
        scratch_shapes=[
            pltpu.VMEM(pressure.shape, bf16),
            pltpu.VMEM((640, LANES), f32),
            pltpu.SemaphoreType.DMA((3,)),
        ],
        compiler_params=GRANT,
        name="spread",
    )(kept(pressure), kept(table))
    got = lax.all_to_all(send.reshape(PARTS, FIVE, 2, LANES), "azim", 0, 0, tiled=True)
    spectrum = pl.pallas_call(
        transform_kernel,
        out_shape=pltpu.VMEM((640, LANES), bf16),
        in_specs=[vmem, vmem],
        out_specs=vmem,
        scratch_shapes=[pltpu.VMEM((640, LANES), f32), pltpu.VMEM((640, LANES), f32)],
        compiler_params=GRANT,
        name="transform",
    )(near(got.reshape(640, LANES)), near(table))
    owned = lax.all_to_all(spectrum.reshape(PARTS, FIVE, 2, LANES), "azim", 0, 0, tiled=True)
    owned = owned.reshape(640, LANES)
    chips = [[2 * x + c for x in range(CHIPS)] for c in range(2)]
    mine = lax.all_to_all(
        jnp.broadcast_to(owned[None], (CHIPS, 640, LANES)), "tm", 0, 0, tiled=True, axis_index_groups=chips
    )
    theirs = lax.ppermute(mine, "tm", [(i, i ^ 1) for i in range(2 * CHIPS)])
    out = jax.ShapeDtypeStruct((2, 2, LANES, 2 * WIDE), f32)
    tile = pltpu.VMEM((2, CHIPS, 2, LANES, LANES), f32)
    steps = (2, CHIPS + 1, 2 * LANES, LANES)
    gram_xx, left, after = pl.pallas_call(
        own_kernel,
        out_shape=(out, pltpu.VMEM((2, 2 * LANES, 2 * ROWS), bf16), pltpu.VMEM(steps, f32)),
        in_specs=[vmem],
        out_specs=(hbm, vmem, vmem),
        scratch_shapes=[tile, pltpu.SemaphoreType.DMA((2, CHIPS))],
        compiler_params=GRANT,
        name="own",
    )(near(mine))
    return pl.pallas_call(
        partner_kernel,
        out_shape=(out, out),
        in_specs=[vmem, vmem, vmem, hbm],
        out_specs=(hbm, hbm),
        scratch_shapes=[
            tile,
            pltpu.VMEM((2, 2, CHIPS, 2, LANES, LANES), f32),
            pltpu.VMEM(steps, f32),
            pltpu.SemaphoreType.DMA((2, CHIPS)),
            pltpu.SemaphoreType.DMA((2, 2, CHIPS)),
        ],
        input_output_aliases={3: 0},
        compiler_params=GRANT,
        name="partner",
    )(near(theirs), near(left), near(after), gram_xx)


def solution(mesh):
    in_specs = (P("azim", None, "tm"),)
    out_specs = (P("azim", None, "tm", None), P("azim", None, "tm", None))
    return jax.shard_map(body, mesh=mesh, in_specs=in_specs, out_specs=out_specs, check_vma=False)
```

```python
import jax
import jax.numpy as jnp
import numpy as np
from jax import lax
from jax.experimental import pallas as pl
from jax.experimental.pallas import tpu as pltpu
from jax.sharding import PartitionSpec as P

THETA = 256
MODES = 128
ROWS = 160
LANES = 128
HALF = 64
PARTS = 64
FIVE = 5
CELL = 2 * FIVE


def make_table():
    b, alo, p, k, ahi, s = np.meshgrid(
        np.arange(2), np.arange(2), np.arange(2), np.arange(64), np.arange(2), np.arange(64), indexing="ij"
    )
    angle = 4 * s + 2 * ahi + alo
    wave = 2 * k + b
    phase = ((angle * wave) % THETA).astype(np.float32) * np.float32(2.0 * np.pi / THETA)
    values = np.where(p == 1, -np.sin(phase), np.cos(phase)) * np.float32(THETA ** (-0.5))
    return values.astype(np.float32).reshape(512, 128).astype(jnp.bfloat16)


def low_lanes(shape):
    return lax.broadcasted_iota(jnp.int32, shape, 1) < HALF


def spread_kernel(x_ref, t_ref, o_ref, table_ref, near_ref, scr, sems):
    fetch = [
        pltpu.make_async_copy(x_ref.at[pl.ds(2 * ahi, 2)], near_ref.at[pl.ds(2 * ahi, 2)], sems.at[ahi])
        for ahi in range(2)
    ]
    fetch.append(pltpu.make_async_copy(t_ref, table_ref, sems.at[2]))
    for copy in fetch:
        copy.start()
    low = low_lanes((ROWS, LANES))
    for ahi in range(2):
        fetch[ahi].wait()
        even = near_ref[2 * ahi].astype(jnp.float32)
        odd = near_ref[2 * ahi + 1].astype(jnp.float32)
        scr[pl.ds(ahi, ROWS, stride=2), :] = jnp.where(low, even, pltpu.roll(odd, HALF, 1))
        scr[pl.ds(2 * ROWS + ahi, ROWS, stride=2), :] = jnp.where(low, pltpu.roll(even, HALF, 1), odd)
    o_ref[...] = scr[...].astype(jnp.bfloat16)
    fetch[2].wait()


def transform_kernel(x_ref, t_ref, o_ref, scr_in, scr_out):
    half = lax.axis_index("azim") // (PARTS // 2)
    one = t_ref[pl.ds(pl.multiple_of(256 * half, 256), 256)]
    two = t_ref[pl.ds(pl.multiple_of(256 * (1 - half), 256), 256)]
    scr_in[...] = x_ref[...].astype(jnp.float32)
    low = low_lanes((LANES, LANES))
    for r5 in range(FIVE):
        field = jnp.concatenate(
            [scr_in[pl.ds(2 * r5 + ahi, PARTS, stride=CELL), :] for ahi in range(2)], axis=0
        ).astype(jnp.bfloat16)
        y = jnp.dot(one, field, preferred_element_type=jnp.float32)
        w = jnp.dot(two, field, preferred_element_type=jnp.float32)
        straight = jnp.where(low, y[0:128], w[128:256])
        crossed = jnp.where(low, w[0:128], y[128:256])
        both = straight + pltpu.roll(crossed, HALF, 1)
        for p in range(2):
            scr_out[pl.ds(2 * r5 + p, PARTS, stride=CELL), :] = both[64 * p : 64 * p + 64]
    o_ref[...] = scr_out[...].astype(jnp.bfloat16)


GAIN = ROWS ** (-0.5)
CHIPS = 4
WIDE = CHIPS * LANES
GRANT = pltpu.CompilerParams(vmem_limit_bytes=16 << 20)


def arrange_kernel(x_ref, o_ref):
    low = low_lanes((2 * ROWS, LANES))
    first = x_ref[0 : 2 * ROWS]
    second = x_ref[2 * ROWS : 4 * ROWS]
    o_ref[0] = jnp.where(low, first, second)
    o_ref[1] = pltpu.roll(jnp.where(low, second, first), HALF, 1)


def blocks_of(left_ref, ref, m):
    for x in range(0, CHIPS, 2):
        rows = jnp.concatenate([ref[x, m], ref[x + 1, m]], axis=1)
        g = jnp.dot(left_ref[m], rows, preferred_element_type=jnp.float32) * jnp.float32(GAIN)
        yield x, g[:, :LANES]
        yield x + 1, g[:, LANES:]


def tile_copy(src, dst, m, x, par, sem):
    at = pl.multiple_of((2 * x + par) * LANES, LANES)
    return pltpu.make_async_copy(src.at[m, x], dst.at[m, :, :, pl.ds(at, LANES)], sem)


def store_tile(ref, m, x, value):
    ref[m, x, 0] = value[:LANES]
    ref[m, x, 1] = value[LANES:]


def own_kernel(mine_ref, xx_ref, left_ref, next_ref, tile, sems):
    tm = lax.axis_index("tm")
    core = lax.rem(tm, 2)
    even = lax.rem(lax.broadcasted_iota(jnp.int32, (2 * ROWS, LANES), 0), 2) == 0

    @pl.loop(0, 2)
    def _(m):
        f = mine_ref[lax.div(tm, 2), m].astype(jnp.float32)
        turned = jnp.where(even, -pltpu.roll(f, 2 * ROWS - 1, 0), pltpu.roll(f, 1, 0))
        left_ref[m, :LANES] = f.T.astype(jnp.bfloat16)
        left_ref[m, LANES:] = turned.T.astype(jnp.bfloat16)
        for x, block in blocks_of(left_ref, mine_ref, m):
            store_tile(tile, m, x, jnp.where(2 * x + core <= tm, block, 0.0))
            tile_copy(tile, xx_ref, m, x, core, sems.at[m, x]).start()
            next_ref[m, x] = pltpu.roll(block, LANES - 1, 1)
        next_ref[m, CHIPS] = jnp.zeros((2 * LANES, LANES), jnp.float32)

    for m in range(2):
        for x in range(CHIPS):
            tile_copy(tile, xx_ref, m, x, core, sems.at[m, x]).wait()


def partner_kernel(theirs_ref, left_ref, next_ref, old_ref, xx_ref, xy_ref, tile, pair, ynext, sems, ysems):
    del old_ref
    tm = lax.axis_index("tm")
    core = lax.rem(tm, 2)
    other = 1 - core
    inner = lax.broadcasted_iota(jnp.int32, (2 * LANES, LANES), 1) < LANES - 1

    @pl.loop(0, 2)
    def _(m):
        for x, block in blocks_of(left_ref, theirs_ref, m):
            keep = 2 * x + other <= tm
            store_tile(tile, m, x, jnp.where(keep, block, 0.0))
            tile_copy(tile, xx_ref, m, x, other, sems.at[m, x]).start()
            shifted = pltpu.roll(block, LANES - 1, 1)
            ynext[m, x] = shifted
            whole = jnp.where(inner, shifted, next_ref[m, x + 1 - core])
            store_tile(pair.at[1], m, x, jnp.where(keep, whole, 0.0))
            tile_copy(pair.at[1], xy_ref, m, x, other, ysems.at[1, m, x]).start()
        ynext[m, CHIPS] = jnp.zeros((2 * LANES, LANES), jnp.float32)
        for x in range(CHIPS):
            whole = jnp.where(inner, next_ref[m, x], ynext[m, x + core])
            store_tile(pair.at[0], m, x, jnp.where(2 * x + core <= tm, whole, 0.0))
            tile_copy(pair.at[0], xy_ref, m, x, core, ysems.at[0, m, x]).start()

    for m in range(2):
        for x in range(CHIPS):
            tile_copy(tile, xx_ref, m, x, other, sems.at[m, x]).wait()
            tile_copy(pair.at[1], xy_ref, m, x, other, ysems.at[1, m, x]).wait()
            tile_copy(pair.at[0], xy_ref, m, x, core, ysems.at[0, m, x]).wait()


def near(array):
    return pltpu.with_memory_space_constraint(array, pltpu.VMEM)


def kept(array):
    return pltpu.with_memory_space_constraint(array, pltpu.HBM)


def body(pressure):
    f32 = jnp.float32
    bf16 = jnp.bfloat16
    vmem = pl.BlockSpec(memory_space=pltpu.VMEM)
    hbm = pl.BlockSpec(memory_space=pl.ANY)
    far = pl.BlockSpec(memory_space=pltpu.HBM)
    table = jnp.asarray(make_table())
    send, table = pl.pallas_call(
        spread_kernel,
        out_shape=(pltpu.VMEM((640, LANES), bf16), pltpu.VMEM(table.shape, bf16)),
        in_specs=[far, far],
        out_specs=(vmem, vmem),
        scratch_shapes=[
            pltpu.VMEM(pressure.shape, bf16),
            pltpu.VMEM((640, LANES), f32),
            pltpu.SemaphoreType.DMA((3,)),
        ],
        compiler_params=GRANT,
        name="spread",
    )(kept(pressure), kept(table))
    got = lax.all_to_all(send.reshape(PARTS, FIVE, 2, LANES), "azim", 0, 0, tiled=True)
    spectrum = pl.pallas_call(
        transform_kernel,
        out_shape=pltpu.VMEM((640, LANES), bf16),
        in_specs=[vmem, vmem],
        out_specs=vmem,
        scratch_shapes=[pltpu.VMEM((640, LANES), f32), pltpu.VMEM((640, LANES), f32)],
        compiler_params=GRANT,
        name="transform",
    )(near(got.reshape(640, LANES)), near(table))
    owned = lax.all_to_all(spectrum.reshape(PARTS, FIVE, 2, LANES), "azim", 0, 0, tiled=True)
    owned = pl.pallas_call(
        arrange_kernel,
        out_shape=pltpu.VMEM((2, 2 * ROWS, LANES), bf16),
        in_specs=[vmem],
        out_specs=vmem,
        compiler_params=GRANT,
        name="arrange",
    )(near(owned.reshape(640, LANES)))
    chips = [[2 * x + c for x in range(CHIPS)] for c in range(2)]
    mine = lax.all_to_all(
        jnp.broadcast_to(owned[None], (CHIPS,) + owned.shape), "tm", 0, 0, tiled=True, axis_index_groups=chips
    )
    theirs = lax.ppermute(mine, "tm", [(i, i ^ 1) for i in range(2 * CHIPS)])
    out = jax.ShapeDtypeStruct((2, 2, LANES, 2 * WIDE), f32)
    tile = pltpu.VMEM((2, CHIPS, 2, LANES, LANES), f32)
    steps = (2, CHIPS + 1, 2 * LANES, LANES)
    gram_xx, left, after = pl.pallas_call(
        own_kernel,
        out_shape=(out, pltpu.VMEM((2, 2 * LANES, 2 * ROWS), bf16), pltpu.VMEM(steps, f32)),
        in_specs=[vmem],
        out_specs=(hbm, vmem, vmem),
        scratch_shapes=[tile, pltpu.SemaphoreType.DMA((2, CHIPS))],
        compiler_params=GRANT,
        name="own",
    )(near(mine))
    return pl.pallas_call(
        partner_kernel,
        out_shape=(out, out),
        in_specs=[vmem, vmem, vmem, hbm],
        out_specs=(hbm, hbm),
        scratch_shapes=[
            tile,
            pltpu.VMEM((2, 2, CHIPS, 2, LANES, LANES), f32),
            pltpu.VMEM(steps, f32),
            pltpu.SemaphoreType.DMA((2, CHIPS)),
            pltpu.SemaphoreType.DMA((2, 2, CHIPS)),
        ],
        input_output_aliases={3: 0},
        compiler_params=GRANT,
        name="partner",
    )(near(theirs), near(left), near(after), gram_xx)


def solution(mesh):
    in_specs = (P("azim", None, "tm"),)
    out_specs = (P("azim", None, "tm", None), P("azim", None, "tm", None))
    return jax.shard_map(body, mesh=mesh, in_specs=in_specs, out_specs=out_specs, check_vma=False)
```

```python
import jax
import jax.numpy as jnp
import numpy as np
from jax import lax
from jax.experimental import pallas as pl
from jax.experimental.pallas import tpu as pltpu
from jax.sharding import PartitionSpec as P

THETA = 256
MODES = 128
ROWS = 160
LANES = 128
HALF = 64
PARTS = 64
FIVE = 5
CELL = 2 * FIVE


def make_table():
    b, alo, p, k, ahi, s = np.meshgrid(
        np.arange(2), np.arange(2), np.arange(2), np.arange(64), np.arange(2), np.arange(64), indexing="ij"
    )
    angle = 4 * s + 2 * ahi + alo
    wave = 2 * k + b
    phase = ((angle * wave) % THETA).astype(np.float32) * np.float32(2.0 * np.pi / THETA)
    values = np.where(p == 1, -np.sin(phase), np.cos(phase)) * np.float32(THETA ** (-0.5))
    return values.astype(np.float32).reshape(512, 128).astype(jnp.bfloat16)


def low_lanes(shape):
    return lax.broadcasted_iota(jnp.int32, shape, 1) < HALF


def spread_kernel(x_ref, t_ref, o_ref, table_ref, near_ref, scr, sems):
    fetch = [
        pltpu.make_async_copy(x_ref.at[pl.ds(2 * ahi, 2)], near_ref.at[pl.ds(2 * ahi, 2)], sems.at[ahi])
        for ahi in range(2)
    ]
    fetch.append(pltpu.make_async_copy(t_ref, table_ref, sems.at[2]))
    for copy in fetch:
        copy.start()
    low = low_lanes((ROWS, LANES))
    for ahi in range(2):
        fetch[ahi].wait()
        even = near_ref[2 * ahi].astype(jnp.float32)
        odd = near_ref[2 * ahi + 1].astype(jnp.float32)
        scr[pl.ds(ahi, ROWS, stride=2), :] = jnp.where(low, even, pltpu.roll(odd, HALF, 1))
        scr[pl.ds(2 * ROWS + ahi, ROWS, stride=2), :] = jnp.where(low, pltpu.roll(even, HALF, 1), odd)
    o_ref[...] = scr[...].astype(jnp.bfloat16)
    fetch[2].wait()


def transform_kernel(x_ref, t_ref, o_ref, scr_in, scr_out):
    half = lax.axis_index("azim") // (PARTS // 2)
    one = t_ref[pl.ds(pl.multiple_of(256 * half, 256), 256)]
    two = t_ref[pl.ds(pl.multiple_of(256 * (1 - half), 256), 256)]
    scr_in[...] = x_ref[...].astype(jnp.float32)
    low = low_lanes((LANES, LANES))
    for r5 in range(FIVE):
        field = jnp.concatenate(
            [scr_in[pl.ds(2 * r5 + ahi, PARTS, stride=CELL), :] for ahi in range(2)], axis=0
        ).astype(jnp.bfloat16)
        y = jnp.dot(one, field, preferred_element_type=jnp.float32)
        w = jnp.dot(two, field, preferred_element_type=jnp.float32)
        straight = jnp.where(low, y[0:128], w[128:256])
        crossed = jnp.where(low, w[0:128], y[128:256])
        both = straight + pltpu.roll(crossed, HALF, 1)
        for p in range(2):
            scr_out[pl.ds(2 * r5 + p, PARTS, stride=CELL), :] = both[64 * p : 64 * p + 64]
    o_ref[...] = scr_out[...].astype(jnp.bfloat16)


GAIN = ROWS ** (-0.5)
CHIPS = 4
WIDE = CHIPS * LANES
GRANT = pltpu.CompilerParams(vmem_limit_bytes=16 << 20)


def arrange_kernel(x_ref, o_ref):
    low = low_lanes((2 * ROWS, LANES))
    first = x_ref[0 : 2 * ROWS]
    second = x_ref[2 * ROWS : 4 * ROWS]
    o_ref[0] = jnp.where(low, first, second)
    o_ref[1] = pltpu.roll(jnp.where(low, second, first), HALF, 1)


def columns_of(left_ref, ref, m, x):
    rows = jnp.concatenate([ref[x, m], ref[x + 1, m]], axis=1)
    g = jnp.dot(left_ref[m], rows, preferred_element_type=jnp.float32) * jnp.float32(GAIN)
    return g[:, :LANES], g[:, LANES:]


def tile_copy(src, dst, m, x, par, sem):
    at = pl.multiple_of((2 * x + par) * LANES, LANES)
    return pltpu.make_async_copy(src.at[m, x], dst.at[m, :, :, pl.ds(at, LANES)], sem)


def store_tile(ref, m, x, value):
    ref[m, x, 0] = value[:LANES]
    ref[m, x, 1] = value[LANES:]


def own_kernel(mine_ref, xx_ref, xy_ref, left_ref, next_ref, tile, zero, sems, zsems):
    tm = lax.axis_index("tm")
    core = lax.rem(tm, 2)
    zero[...] = jnp.zeros(zero.shape, jnp.float32)

    def blank(j, act):
        @pl.when(j > tm)
        def _():
            for i, dst in enumerate((xx_ref, xy_ref)):
                act(pltpu.make_async_copy(zero, dst.at[:, :, :, pl.ds(j * LANES, LANES)], zsems.at[i, j]))

    def tiles(m, x, act):
        @pl.when(2 * x + core <= tm)
        def _():
            act(tile_copy(tile, xx_ref, m, x, core, sems.at[m, x]))

    for j in range(1, 2 * CHIPS):
        blank(j, lambda copy: copy.start())
    even = lax.rem(lax.broadcasted_iota(jnp.int32, (2 * ROWS, LANES), 0), 2) == 0

    @pl.loop(0, 2)
    def _(m):
        f = mine_ref[lax.div(tm, 2), m].astype(jnp.float32)
        turned = jnp.where(even, -pltpu.roll(f, 2 * ROWS - 1, 0), pltpu.roll(f, 1, 0))
        left_ref[m, :LANES] = f.T.astype(jnp.bfloat16)
        left_ref[m, LANES:] = turned.T.astype(jnp.bfloat16)
        for first in range(0, CHIPS, 2):

            @pl.when(2 * first + core <= tm)
            def _():
                for i, block in enumerate(columns_of(left_ref, mine_ref, m, first)):
                    store_tile(tile, m, first + i, block)
                    tiles(m, first + i, lambda copy: copy.start())
                    next_ref[m, first + i] = pltpu.roll(block, LANES - 1, 1)

    for m in range(2):
        for x in range(CHIPS):
            tiles(m, x, lambda copy: copy.wait())
    for j in range(1, 2 * CHIPS):
        blank(j, lambda copy: copy.wait())


def partner_kernel(theirs_ref, left_ref, next_ref, old_xx, old_xy, xx_ref, xy_ref, tile, pair, ynext, sems, ysems):
    del old_xx, old_xy
    tm = lax.axis_index("tm")
    core = lax.rem(tm, 2)
    other = 1 - core
    inner = lax.broadcasted_iota(jnp.int32, (2 * LANES, LANES), 1) < LANES - 1

    def other_tiles(m, x, act):
        @pl.when(2 * x + other <= tm)
        def _():
            act(tile_copy(tile, xx_ref, m, x, other, sems.at[m, x]))
            act(tile_copy(pair.at[1], xy_ref, m, x, other, ysems.at[1, m, x]))

    def own_tile(m, x):
        return tile_copy(pair.at[0], xy_ref, m, x, core, ysems.at[0, m, x])

    @pl.loop(0, 2)
    def _(m):
        for first in range(0, CHIPS, 2):

            @pl.when(2 * first + other <= tm + 1)
            def _():
                for i, block in enumerate(columns_of(left_ref, theirs_ref, m, first)):
                    x = first + i
                    store_tile(tile, m, x, block)
                    shifted = pltpu.roll(block, LANES - 1, 1)
                    ynext[m, x] = shifted
                    store_tile(pair.at[1], m, x, jnp.where(inner, shifted, next_ref[m, x + 1 - core]))
                    other_tiles(m, x, lambda copy: copy.start())

        ynext[m, CHIPS] = jnp.zeros((2 * LANES, LANES), jnp.float32)
        for x in range(CHIPS):

            @pl.when(2 * x + core <= tm)
            def _():
                store_tile(pair.at[0], m, x, jnp.where(inner, next_ref[m, x], ynext[m, x + core]))
                own_tile(m, x).start()

    for m in range(2):
        for x in range(CHIPS):
            other_tiles(m, x, lambda copy: copy.wait())

            @pl.when(2 * x + core <= tm)
            def _():
                own_tile(m, x).wait()


def near(array):
    return pltpu.with_memory_space_constraint(array, pltpu.VMEM)


def kept(array):
    return pltpu.with_memory_space_constraint(array, pltpu.HBM)


def body(pressure):
    f32 = jnp.float32
    bf16 = jnp.bfloat16
    vmem = pl.BlockSpec(memory_space=pltpu.VMEM)
    hbm = pl.BlockSpec(memory_space=pl.ANY)
    far = pl.BlockSpec(memory_space=pltpu.HBM)
    table = jnp.asarray(make_table())
    send, table = pl.pallas_call(
        spread_kernel,
        out_shape=(pltpu.VMEM((640, LANES), bf16), pltpu.VMEM(table.shape, bf16)),
        in_specs=[far, far],
        out_specs=(vmem, vmem),
        scratch_shapes=[
            pltpu.VMEM(pressure.shape, bf16),
            pltpu.VMEM((640, LANES), f32),
            pltpu.SemaphoreType.DMA((3,)),
        ],
        compiler_params=GRANT,
        name="spread",
    )(kept(pressure), kept(table))
    got = lax.all_to_all(send.reshape(PARTS, FIVE, 2, LANES), "azim", 0, 0, tiled=True)
    spectrum = pl.pallas_call(
        transform_kernel,
        out_shape=pltpu.VMEM((640, LANES), bf16),
        in_specs=[vmem, vmem],
        out_specs=vmem,
        scratch_shapes=[pltpu.VMEM((640, LANES), f32), pltpu.VMEM((640, LANES), f32)],
        compiler_params=GRANT,
        name="transform",
    )(near(got.reshape(640, LANES)), near(table))
    owned = lax.all_to_all(spectrum.reshape(PARTS, FIVE, 2, LANES), "azim", 0, 0, tiled=True)
    owned = pl.pallas_call(
        arrange_kernel,
        out_shape=pltpu.VMEM((2, 2 * ROWS, LANES), bf16),
        in_specs=[vmem],
        out_specs=vmem,
        compiler_params=GRANT,
        name="arrange",
    )(near(owned.reshape(640, LANES)))
    chips = [[2 * x + c for x in range(CHIPS)] for c in range(2)]
    mine = lax.all_to_all(
        jnp.broadcast_to(owned[None], (CHIPS,) + owned.shape), "tm", 0, 0, tiled=True, axis_index_groups=chips
    )
    theirs = lax.ppermute(mine, "tm", [(i, i ^ 1) for i in range(2 * CHIPS)])
    out = jax.ShapeDtypeStruct((2, 2, LANES, 2 * WIDE), f32)
    tile = pltpu.VMEM((2, CHIPS, 2, LANES, LANES), f32)
    steps = (2, CHIPS + 1, 2 * LANES, LANES)
    gram_xx, gram_xy, left, after = pl.pallas_call(
        own_kernel,
        out_shape=(out, out, pltpu.VMEM((2, 2 * LANES, 2 * ROWS), bf16), pltpu.VMEM(steps, f32)),
        in_specs=[vmem],
        out_specs=(hbm, hbm, vmem, vmem),
        scratch_shapes=[
            tile,
            pltpu.VMEM((2, 2, LANES, LANES), f32),
            pltpu.SemaphoreType.DMA((2, CHIPS)),
            pltpu.SemaphoreType.DMA((2, 2 * CHIPS)),
        ],
        compiler_params=GRANT,
        name="own",
    )(near(mine))
    return pl.pallas_call(
        partner_kernel,
        out_shape=(out, out),
        in_specs=[vmem, vmem, vmem, hbm, hbm],
        out_specs=(hbm, hbm),
        scratch_shapes=[
            tile,
            pltpu.VMEM((2, 2, CHIPS, 2, LANES, LANES), f32),
            pltpu.VMEM(steps, f32),
            pltpu.SemaphoreType.DMA((2, CHIPS)),
            pltpu.SemaphoreType.DMA((2, 2, CHIPS)),
        ],
        input_output_aliases={3: 0, 4: 1},
        compiler_params=GRANT,
        name="partner",
    )(near(theirs), near(left), near(after), gram_xx, gram_xy)


def solution(mesh):
    in_specs = (P("azim", None, "tm"),)
    out_specs = (P("azim", None, "tm", None), P("azim", None, "tm", None))
    return jax.shard_map(body, mesh=mesh, in_specs=in_specs, out_specs=out_specs, check_vma=False)
```

```python
import jax
import jax.numpy as jnp
import numpy as np
from jax import lax
from jax.experimental import pallas as pl
from jax.experimental.pallas import tpu as pltpu
from jax.sharding import PartitionSpec as P

THETA = 256
MODES = 128
ROWS = 160
LANES = 128
HALF = 64
PARTS = 64
FIVE = 5
CELL = 2 * FIVE


def make_table():
    b, alo, p, k, ahi, s = np.meshgrid(
        np.arange(2), np.arange(2), np.arange(2), np.arange(64), np.arange(2), np.arange(64), indexing="ij"
    )
    angle = 4 * s + 2 * ahi + alo
    wave = 2 * k + b
    phase = ((angle * wave) % THETA).astype(np.float32) * np.float32(2.0 * np.pi / THETA)
    values = np.where(p == 1, -np.sin(phase), np.cos(phase)) * np.float32(THETA ** (-0.5))
    return values.astype(np.float32).reshape(512, 128).astype(jnp.bfloat16)


def low_lanes(shape):
    return lax.broadcasted_iota(jnp.int32, shape, 1) < HALF


def spread_kernel(x_ref, t_ref, o_ref, table_ref, near_ref, scr, sems):
    fetch = [
        pltpu.make_async_copy(x_ref.at[pl.ds(2 * ahi, 2)], near_ref.at[pl.ds(2 * ahi, 2)], sems.at[ahi])
        for ahi in range(2)
    ]
    fetch.append(pltpu.make_async_copy(t_ref, table_ref, sems.at[2]))
    for copy in fetch:
        copy.start()
    low = low_lanes((ROWS, LANES))
    for ahi in range(2):
        fetch[ahi].wait()
        even = near_ref[2 * ahi].astype(jnp.float32)
        odd = near_ref[2 * ahi + 1].astype(jnp.float32)
        scr[pl.ds(ahi, ROWS, stride=2), :] = jnp.where(low, even, pltpu.roll(odd, HALF, 1))
        scr[pl.ds(2 * ROWS + ahi, ROWS, stride=2), :] = jnp.where(low, pltpu.roll(even, HALF, 1), odd)
    o_ref[...] = scr[...].astype(jnp.bfloat16)
    fetch[2].wait()


def transform_kernel(x_ref, t_ref, o_ref, scr_in, scr_out):
    half = lax.axis_index("azim") // (PARTS // 2)
    one = t_ref[pl.ds(pl.multiple_of(256 * half, 256), 256)]
    two = t_ref[pl.ds(pl.multiple_of(256 * (1 - half), 256), 256)]
    scr_in[...] = x_ref[...].astype(jnp.float32)
    low = low_lanes((LANES, LANES))
    for r5 in range(FIVE):
        field = jnp.concatenate(
            [scr_in[pl.ds(2 * r5 + ahi, PARTS, stride=CELL), :] for ahi in range(2)], axis=0
        ).astype(jnp.bfloat16)
        y = jnp.dot(one, field, preferred_element_type=jnp.float32)
        w = jnp.dot(two, field, preferred_element_type=jnp.float32)
        straight = jnp.where(low, y[0:128], w[128:256])
        crossed = jnp.where(low, w[0:128], y[128:256])
        both = straight + pltpu.roll(crossed, HALF, 1)
        for p in range(2):
            scr_out[pl.ds(2 * r5 + p, PARTS, stride=CELL), :] = both[64 * p : 64 * p + 64]
    o_ref[...] = scr_out[...].astype(jnp.bfloat16)


GAIN = ROWS ** (-0.5)
CHIPS = 4
WIDE = CHIPS * LANES
GRANT = pltpu.CompilerParams(vmem_limit_bytes=16 << 20)


def arrange_kernel(x_ref, o_ref):
    low = low_lanes((2 * ROWS, LANES))
    first = x_ref[0 : 2 * ROWS]
    second = x_ref[2 * ROWS : 4 * ROWS]
    o_ref[0] = jnp.where(low, first, second)
    o_ref[1] = pltpu.roll(jnp.where(low, second, first), HALF, 1)


def columns_of(left_ref, ref, m, x):
    rows = jnp.concatenate([ref[x, m], ref[x + 1, m]], axis=1)
    g = jnp.dot(left_ref[m], rows, preferred_element_type=jnp.float32) * jnp.float32(GAIN)
    return g[:, :LANES], g[:, LANES:]


def tile_copy(src, dst, m, x, par, sem):
    at = pl.multiple_of((2 * x + par) * LANES, LANES)
    return pltpu.make_async_copy(src.at[m, x], dst.at[m, :, :, pl.ds(at, LANES)], sem)


def store_tile(ref, m, x, value):
    ref[m, x, 0] = value[:LANES]
    ref[m, x, 1] = value[LANES:]


def own_step(mine_ref, xx_ref, xy_ref, left_ref, next_ref, tile, zero, sems, zsems):
    tm = lax.axis_index("tm")
    core = lax.rem(tm, 2)
    zero[...] = jnp.zeros(zero.shape, jnp.float32)

    def blank(dst, j, sem):
        at = pl.multiple_of(j * LANES, LANES)
        return pltpu.make_async_copy(zero, dst.at[:, :, :, pl.ds(at, LANES)], sem)

    def blanks(act):
        @pl.loop(tm + 1, 2 * CHIPS)
        def _(j):
            act(blank(xy_ref, j, zsems.at[0, j]))

        @pl.loop(lax.div(tm + 1, 2), CHIPS)
        def _(x):
            act(blank(xx_ref, 2 * x + 1 - core, zsems.at[1, x]))

    blanks(lambda copy: copy.start())
    even = lax.rem(lax.broadcasted_iota(jnp.int32, (2 * ROWS, LANES), 0), 2) == 0

    @pl.loop(0, 2)
    def _(m):
        f = mine_ref[lax.div(tm, 2), m].astype(jnp.float32)
        turned = jnp.where(even, -pltpu.roll(f, 2 * ROWS - 1, 0), pltpu.roll(f, 1, 0))
        left_ref[m, :LANES] = f.T.astype(jnp.bfloat16)
        left_ref[m, LANES:] = turned.T.astype(jnp.bfloat16)
        for first in range(0, CHIPS, 2):
            for i, block in enumerate(columns_of(left_ref, mine_ref, m, first)):
                x = first + i
                store_tile(tile, m, x, jnp.where(2 * x + core <= tm, block, 0.0))
                tile_copy(tile, xx_ref, m, x, core, sems.at[m, x]).start()
                next_ref[m, x] = pltpu.roll(block, LANES - 1, 1)
        next_ref[m, CHIPS] = jnp.zeros((2 * LANES, LANES), jnp.float32)

    for m in range(2):
        for x in range(CHIPS):
            tile_copy(tile, xx_ref, m, x, core, sems.at[m, x]).wait()
    blanks(lambda copy: copy.wait())


def ahead_kernel(mine_ref, same_ref, *rest):
    del same_ref

    @pl.when(lax.rem(lax.axis_index("tm"), 2) == 1)
    def _():
        own_step(mine_ref, *rest)


def behind_kernel(mine_ref, old_xx, old_xy, old_left, old_next, *rest):
    del old_xx, old_xy, old_left, old_next

    @pl.when(lax.rem(lax.axis_index("tm"), 2) == 0)
    def _():
        own_step(mine_ref, *rest)


def partner_kernel(theirs_ref, left_ref, next_ref, old_xx, old_xy, xx_ref, xy_ref, tile, pair, ynext, sems, ysems):
    del old_xx, old_xy
    tm = lax.axis_index("tm")
    core = lax.rem(tm, 2)
    other = 1 - core
    inner = lax.broadcasted_iota(jnp.int32, (2 * LANES, LANES), 1) < LANES - 1

    def own_tile(m, x):
        return tile_copy(pair.at[0], xy_ref, m, x, core, ysems.at[0, m, x])

    @pl.loop(0, 2)
    def _(m):
        for first in range(0, CHIPS, 2):

            @pl.when(2 * first + other <= tm + 1)
            def _():
                for i, block in enumerate(columns_of(left_ref, theirs_ref, m, first)):
                    x = first + i
                    store_tile(tile, m, x, block)
                    shifted = pltpu.roll(block, LANES - 1, 1)
                    ynext[m, x] = shifted
                    store_tile(pair.at[1], m, x, jnp.where(inner, shifted, next_ref[m, x + 1 - core]))

                    @pl.when(2 * x + other <= tm)
                    def _():
                        tile_copy(tile, xx_ref, m, x, other, sems.at[m, x]).start()
                        tile_copy(pair.at[1], xy_ref, m, x, other, ysems.at[1, m, x]).start()

        ynext[m, CHIPS] = jnp.zeros((2 * LANES, LANES), jnp.float32)
        for x in range(CHIPS):

            @pl.when(2 * x + core <= tm)
            def _():
                store_tile(pair.at[0], m, x, jnp.where(inner, next_ref[m, x], ynext[m, x + core]))
                own_tile(m, x).start()

    @pl.loop(0, lax.div(tm + 1, 2))
    def _(x):
        for m in range(2):
            tile_copy(tile, xx_ref, m, x, other, sems.at[m, x]).wait()
            tile_copy(pair.at[1], xy_ref, m, x, other, ysems.at[1, m, x]).wait()

    @pl.loop(0, lax.div(tm, 2) + 1)
    def _(x):
        for m in range(2):
            own_tile(m, x).wait()


def near(array):
    return pltpu.with_memory_space_constraint(array, pltpu.VMEM)


def kept(array):
    return pltpu.with_memory_space_constraint(array, pltpu.HBM)


def body(pressure):
    f32 = jnp.float32
    bf16 = jnp.bfloat16
    vmem = pl.BlockSpec(memory_space=pltpu.VMEM)
    hbm = pl.BlockSpec(memory_space=pl.ANY)
    far = pl.BlockSpec(memory_space=pltpu.HBM)
    table = jnp.asarray(make_table())
    send, table = pl.pallas_call(
        spread_kernel,
        out_shape=(pltpu.VMEM((640, LANES), bf16), pltpu.VMEM(table.shape, bf16)),
        in_specs=[far, far],
        out_specs=(vmem, vmem),
        scratch_shapes=[
            pltpu.VMEM(pressure.shape, bf16),
            pltpu.VMEM((640, LANES), f32),
            pltpu.SemaphoreType.DMA((3,)),
        ],
        compiler_params=GRANT,
        name="spread",
    )(kept(pressure), kept(table))
    got = lax.all_to_all(send.reshape(PARTS, FIVE, 2, LANES), "azim", 0, 0, tiled=True)
    spectrum = pl.pallas_call(
        transform_kernel,
        out_shape=pltpu.VMEM((640, LANES), bf16),
        in_specs=[vmem, vmem],
        out_specs=vmem,
        scratch_shapes=[pltpu.VMEM((640, LANES), f32), pltpu.VMEM((640, LANES), f32)],
        compiler_params=GRANT,
        name="transform",
    )(near(got.reshape(640, LANES)), near(table))
    owned = lax.all_to_all(spectrum.reshape(PARTS, FIVE, 2, LANES), "azim", 0, 0, tiled=True)
    owned = pl.pallas_call(
        arrange_kernel,
        out_shape=pltpu.VMEM((2, 2 * ROWS, LANES), bf16),
        in_specs=[vmem],
        out_specs=vmem,
        compiler_params=GRANT,
        name="arrange",
    )(near(owned.reshape(640, LANES)))
    chips = [[2 * x + c for x in range(CHIPS)] for c in range(2)]
    mine = lax.all_to_all(
        jnp.broadcast_to(owned[None], (CHIPS,) + owned.shape), "tm", 0, 0, tiled=True, axis_index_groups=chips
    )
    out = jax.ShapeDtypeStruct((2, 2, LANES, 2 * WIDE), f32)
    tile = pltpu.VMEM((2, CHIPS, 2, LANES, LANES), f32)
    steps = (2, CHIPS + 1, 2 * LANES, LANES)
    results = (out, out, pltpu.VMEM((2, 2 * LANES, 2 * ROWS), bf16), pltpu.VMEM(steps, f32))
    scratch = [
        tile,
        pltpu.VMEM((2, 2, LANES, LANES), f32),
        pltpu.SemaphoreType.DMA((2, CHIPS)),
        pltpu.SemaphoreType.DMA((2, 2 * CHIPS)),
    ]
    mine, gram_xx, gram_xy, left, after = pl.pallas_call(
        ahead_kernel,
        out_shape=(pltpu.VMEM(mine.shape, bf16),) + results,
        in_specs=[vmem],
        out_specs=(vmem, hbm, hbm, vmem, vmem),
        scratch_shapes=scratch,
        input_output_aliases={0: 0},
        compiler_params=GRANT,
        name="ahead",
    )(near(mine))
    theirs = lax.ppermute(mine, "tm", [(i, i ^ 1) for i in range(2 * CHIPS)])
    gram_xx, gram_xy, left, after = pl.pallas_call(
        behind_kernel,
        out_shape=results,
        in_specs=[vmem, hbm, hbm, vmem, vmem],
        out_specs=(hbm, hbm, vmem, vmem),
        scratch_shapes=scratch,
        input_output_aliases={1: 0, 2: 1, 3: 2, 4: 3},
        compiler_params=GRANT,
        name="behind",
    )(near(mine), gram_xx, gram_xy, near(left), near(after))
    return pl.pallas_call(
        partner_kernel,
        out_shape=(out, out),
        in_specs=[vmem, vmem, vmem, hbm, hbm],
        out_specs=(hbm, hbm),
        scratch_shapes=[
            tile,
            pltpu.VMEM((2, 2, CHIPS, 2, LANES, LANES), f32),
            pltpu.VMEM(steps, f32),
            pltpu.SemaphoreType.DMA((2, CHIPS)),
            pltpu.SemaphoreType.DMA((2, 2, CHIPS)),
        ],
        input_output_aliases={3: 0, 4: 1},
        compiler_params=GRANT,
        name="partner",
    )(near(theirs), near(left), near(after), gram_xx, gram_xy)


def solution(mesh):
    in_specs = (P("azim", None, "tm"),)
    out_specs = (P("azim", None, "tm", None), P("azim", None, "tm", None))
    return jax.shard_map(body, mesh=mesh, in_specs=in_specs, out_specs=out_specs, check_vma=False)
```

```python
import jax
import jax.numpy as jnp
import numpy as np
from jax import lax
from jax.experimental import pallas as pl
from jax.experimental.pallas import tpu as pltpu
from jax.sharding import PartitionSpec as P

THETA = 256
MODES = 128
ROWS = 160
LANES = 128
HALF = 64
PARTS = 64
FIVE = 5
CELL = 2 * FIVE


def make_table():
    b, alo, p, k, ahi, s = np.meshgrid(
        np.arange(2), np.arange(2), np.arange(2), np.arange(64), np.arange(2), np.arange(64), indexing="ij"
    )
    angle = 4 * s + 2 * ahi + alo
    wave = 2 * k + b
    phase = ((angle * wave) % THETA).astype(np.float32) * np.float32(2.0 * np.pi / THETA)
    values = np.where(p == 1, -np.sin(phase), np.cos(phase)) * np.float32(THETA ** (-0.5))
    return values.astype(np.float32).reshape(512, 128).astype(jnp.bfloat16)


def low_lanes(shape):
    return lax.broadcasted_iota(jnp.int32, shape, 1) < HALF


def spread_kernel(x_ref, t_ref, o_ref, table_ref, near_ref, scr, sems):
    fetch = [
        pltpu.make_async_copy(x_ref.at[pl.ds(2 * ahi, 2)], near_ref.at[pl.ds(2 * ahi, 2)], sems.at[ahi])
        for ahi in range(2)
    ]
    fetch.append(pltpu.make_async_copy(t_ref, table_ref, sems.at[2]))
    for copy in fetch:
        copy.start()
    low = low_lanes((ROWS, LANES))
    for ahi in range(2):
        fetch[ahi].wait()
        even = near_ref[2 * ahi].astype(jnp.float32)
        odd = near_ref[2 * ahi + 1].astype(jnp.float32)
        scr[pl.ds(ahi, ROWS, stride=2), :] = jnp.where(low, even, pltpu.roll(odd, HALF, 1))
        scr[pl.ds(2 * ROWS + ahi, ROWS, stride=2), :] = jnp.where(low, pltpu.roll(even, HALF, 1), odd)
    o_ref[...] = scr[...].astype(jnp.bfloat16)
    fetch[2].wait()


def transform_kernel(x_ref, t_ref, o_ref, scr_in, scr_out):
    half = lax.axis_index("azim") // (PARTS // 2)
    one = t_ref[pl.ds(pl.multiple_of(256 * half, 256), 256)]
    two = t_ref[pl.ds(pl.multiple_of(256 * (1 - half), 256), 256)]
    scr_in[...] = x_ref[...].astype(jnp.float32)
    low = low_lanes((LANES, LANES))
    for r5 in range(FIVE):
        field = jnp.concatenate(
            [scr_in[pl.ds(2 * r5 + ahi, PARTS, stride=CELL), :] for ahi in range(2)], axis=0
        ).astype(jnp.bfloat16)
        y = jnp.dot(one, field, preferred_element_type=jnp.float32)
        w = jnp.dot(two, field, preferred_element_type=jnp.float32)
        straight = jnp.where(low, y[0:128], w[128:256])
        crossed = jnp.where(low, w[0:128], y[128:256])
        both = straight + pltpu.roll(crossed, HALF, 1)
        for p in range(2):
            scr_out[pl.ds(2 * r5 + p, PARTS, stride=CELL), :] = both[64 * p : 64 * p + 64]
    o_ref[...] = scr_out[...].astype(jnp.bfloat16)


GAIN = ROWS ** (-0.5)
CHIPS = 4
WIDE = CHIPS * LANES
GRANT = pltpu.CompilerParams(vmem_limit_bytes=16 << 20)


def arrange_kernel(x_ref, o_ref):
    low = low_lanes((2 * ROWS, LANES))
    first = x_ref[0 : 2 * ROWS]
    second = x_ref[2 * ROWS : 4 * ROWS]
    o_ref[0] = jnp.where(low, first, second)
    o_ref[1] = pltpu.roll(jnp.where(low, second, first), HALF, 1)


def columns_of(left_ref, ref, m, x):
    rows = jnp.concatenate([ref[x, m], ref[x + 1, m]], axis=1)
    g = jnp.dot(left_ref[m], rows, preferred_element_type=jnp.float32) * jnp.float32(GAIN)
    return g[:, :LANES], g[:, LANES:]


def tile_copy(src, dst, m, x, par, sem):
    at = pl.multiple_of((2 * x + par) * LANES, LANES)
    return pltpu.make_async_copy(src.at[x, m], dst.at[m, :, :, pl.ds(at, LANES)], sem)


def both_copy(src, dst, x, par, sem):
    at = pl.multiple_of((2 * x + par) * LANES, LANES)
    return pltpu.make_async_copy(src.at[x], dst.at[:, :, :, pl.ds(at, LANES)], sem)


def store_tile(ref, m, x, value):
    ref[x, m, 0] = value[:LANES]
    ref[x, m, 1] = value[LANES:]


def own_step(mine_ref, xx_ref, xy_ref, left_ref, next_ref, tile, zero, sems, zsems):
    tm = lax.axis_index("tm")
    core = lax.rem(tm, 2)
    zero[...] = jnp.zeros(zero.shape, jnp.float32)

    def blank(dst, j, sem):
        at = pl.multiple_of(j * LANES, LANES)
        return pltpu.make_async_copy(zero, dst.at[:, :, :, pl.ds(at, LANES)], sem)

    def blanks(act):
        @pl.loop(tm + 1, 2 * CHIPS)
        def _(j):
            act(blank(xy_ref, j, zsems.at[0, j]))

        @pl.loop(lax.div(tm + 1, 2), CHIPS)
        def _(x):
            act(blank(xx_ref, 2 * x + 1 - core, zsems.at[1, x]))

    blanks(lambda copy: copy.start())
    even = lax.rem(lax.broadcasted_iota(jnp.int32, (2 * ROWS, LANES), 0), 2) == 0

    @pl.loop(0, 2)
    def _(m):
        f = mine_ref[lax.div(tm, 2), m].astype(jnp.float32)
        turned = jnp.where(even, -pltpu.roll(f, 2 * ROWS - 1, 0), pltpu.roll(f, 1, 0))
        left_ref[m, :LANES] = f.T.astype(jnp.bfloat16)
        left_ref[m, LANES:] = turned.T.astype(jnp.bfloat16)
        for first in range(0, CHIPS, 2):
            for i, block in enumerate(columns_of(left_ref, mine_ref, m, first)):
                x = first + i
                store_tile(tile, m, x, jnp.where(2 * x + core <= tm, block, 0.0))
                tile_copy(tile, xx_ref, m, x, core, sems.at[m, x]).start()
                next_ref[m, x] = pltpu.roll(block, LANES - 1, 1)
        next_ref[m, CHIPS] = jnp.zeros((2 * LANES, LANES), jnp.float32)

    for m in range(2):
        for x in range(CHIPS):
            tile_copy(tile, xx_ref, m, x, core, sems.at[m, x]).wait()
    blanks(lambda copy: copy.wait())


def ahead_kernel(mine_ref, same_ref, *rest):
    del same_ref

    @pl.when(lax.rem(lax.axis_index("tm"), 2) == 1)
    def _():
        own_step(mine_ref, *rest)


def behind_kernel(mine_ref, old_xx, old_xy, old_left, old_next, *rest):
    del old_xx, old_xy, old_left, old_next

    @pl.when(lax.rem(lax.axis_index("tm"), 2) == 0)
    def _():
        own_step(mine_ref, *rest)


def partner_kernel(theirs_ref, left_ref, next_ref, old_xx, old_xy, xx_ref, xy_ref, tile, pair, ynext, sems, ysems):
    del old_xx, old_xy
    tm = lax.axis_index("tm")
    core = lax.rem(tm, 2)
    other = 1 - core
    inner = lax.broadcasted_iota(jnp.int32, (2 * LANES, LANES), 1) < LANES - 1

    ynext[:, CHIPS] = jnp.zeros((2, 2 * LANES, LANES), jnp.float32)
    for first in range(0, CHIPS, 2):

        @pl.when(2 * first + other <= tm + 1)
        def _():
            for m in range(2):
                for i, block in enumerate(columns_of(left_ref, theirs_ref, m, first)):
                    x = first + i
                    store_tile(tile, m, x, block)
                    shifted = pltpu.roll(block, LANES - 1, 1)
                    ynext[m, x] = shifted
                    store_tile(pair.at[1], m, x, jnp.where(inner, shifted, next_ref[m, x + 1 - core]))
            for x in range(first, first + 2):

                @pl.when(2 * x + other <= tm)
                def _():
                    both_copy(tile, xx_ref, x, other, sems.at[x]).start()
                    both_copy(pair.at[1], xy_ref, x, other, ysems.at[1, x]).start()

    for x in range(CHIPS):

        @pl.when(2 * x + core <= tm)
        def _():
            for m in range(2):
                store_tile(pair.at[0], m, x, jnp.where(inner, next_ref[m, x], ynext[m, x + core]))
            both_copy(pair.at[0], xy_ref, x, core, ysems.at[0, x]).start()

    @pl.loop(0, lax.div(tm + 1, 2))
    def _(x):
        both_copy(tile, xx_ref, x, other, sems.at[x]).wait()
        both_copy(pair.at[1], xy_ref, x, other, ysems.at[1, x]).wait()

    @pl.loop(0, lax.div(tm, 2) + 1)
    def _(x):
        both_copy(pair.at[0], xy_ref, x, core, ysems.at[0, x]).wait()


def near(array):
    return pltpu.with_memory_space_constraint(array, pltpu.VMEM)


def kept(array):
    return pltpu.with_memory_space_constraint(array, pltpu.HBM)


def body(pressure):
    f32 = jnp.float32
    bf16 = jnp.bfloat16
    vmem = pl.BlockSpec(memory_space=pltpu.VMEM)
    hbm = pl.BlockSpec(memory_space=pl.ANY)
    far = pl.BlockSpec(memory_space=pltpu.HBM)
    table = jnp.asarray(make_table())
    send, table = pl.pallas_call(
        spread_kernel,
        out_shape=(pltpu.VMEM((640, LANES), bf16), pltpu.VMEM(table.shape, bf16)),
        in_specs=[far, far],
        out_specs=(vmem, vmem),
        scratch_shapes=[
            pltpu.VMEM(pressure.shape, bf16),
            pltpu.VMEM((640, LANES), f32),
            pltpu.SemaphoreType.DMA((3,)),
        ],
        compiler_params=GRANT,
        name="spread",
    )(kept(pressure), kept(table))
    got = lax.all_to_all(send.reshape(PARTS, FIVE, 2, LANES), "azim", 0, 0, tiled=True)
    spectrum = pl.pallas_call(
        transform_kernel,
        out_shape=pltpu.VMEM((640, LANES), bf16),
        in_specs=[vmem, vmem],
        out_specs=vmem,
        scratch_shapes=[pltpu.VMEM((640, LANES), f32), pltpu.VMEM((640, LANES), f32)],
        compiler_params=GRANT,
        name="transform",
    )(near(got.reshape(640, LANES)), near(table))
    owned = lax.all_to_all(spectrum.reshape(PARTS, FIVE, 2, LANES), "azim", 0, 0, tiled=True)
    owned = pl.pallas_call(
        arrange_kernel,
        out_shape=pltpu.VMEM((2, 2 * ROWS, LANES), bf16),
        in_specs=[vmem],
        out_specs=vmem,
        compiler_params=GRANT,
        name="arrange",
    )(near(owned.reshape(640, LANES)))
    chips = [[2 * x + c for x in range(CHIPS)] for c in range(2)]
    mine = lax.all_to_all(
        jnp.broadcast_to(owned[None], (CHIPS,) + owned.shape), "tm", 0, 0, tiled=True, axis_index_groups=chips
    )
    out = jax.ShapeDtypeStruct((2, 2, LANES, 2 * WIDE), f32)
    tile = pltpu.VMEM((CHIPS, 2, 2, LANES, LANES), f32)
    steps = (2, CHIPS + 1, 2 * LANES, LANES)
    results = (out, out, pltpu.VMEM((2, 2 * LANES, 2 * ROWS), bf16), pltpu.VMEM(steps, f32))
    scratch = [
        tile,
        pltpu.VMEM((2, 2, LANES, LANES), f32),
        pltpu.SemaphoreType.DMA((2, CHIPS)),
        pltpu.SemaphoreType.DMA((2, 2 * CHIPS)),
    ]
    mine, gram_xx, gram_xy, left, after = pl.pallas_call(
        ahead_kernel,
        out_shape=(pltpu.VMEM(mine.shape, bf16),) + results,
        in_specs=[vmem],
        out_specs=(vmem, hbm, hbm, vmem, vmem),
        scratch_shapes=scratch,
        input_output_aliases={0: 0},
        compiler_params=GRANT,
        name="ahead",
    )(near(mine))
    theirs = lax.ppermute(mine, "tm", [(i, i ^ 1) for i in range(2 * CHIPS)])
    gram_xx, gram_xy, left, after = pl.pallas_call(
        behind_kernel,
        out_shape=results,
        in_specs=[vmem, hbm, hbm, vmem, vmem],
        out_specs=(hbm, hbm, vmem, vmem),
        scratch_shapes=scratch,
        input_output_aliases={1: 0, 2: 1, 3: 2, 4: 3},
        compiler_params=GRANT,
        name="behind",
    )(near(mine), gram_xx, gram_xy, near(left), near(after))
    return pl.pallas_call(
        partner_kernel,
        out_shape=(out, out),
        in_specs=[vmem, vmem, vmem, hbm, hbm],
        out_specs=(hbm, hbm),
        scratch_shapes=[
            tile,
            pltpu.VMEM((2, CHIPS, 2, 2, LANES, LANES), f32),
            pltpu.VMEM(steps, f32),
            pltpu.SemaphoreType.DMA((CHIPS,)),
            pltpu.SemaphoreType.DMA((2, CHIPS)),
        ],
        input_output_aliases={3: 0, 4: 1},
        compiler_params=GRANT,
        name="partner",
    )(near(theirs), near(left), near(after), gram_xx, gram_xy)


def solution(mesh):
    in_specs = (P("azim", None, "tm"),)
    out_specs = (P("azim", None, "tm", None), P("azim", None, "tm", None))
    return jax.shard_map(body, mesh=mesh, in_specs=in_specs, out_specs=out_specs, check_vma=False)
```

```python
import jax
import jax.numpy as jnp
import numpy as np
from jax import lax
from jax.experimental import pallas as pl
from jax.experimental.pallas import tpu as pltpu
from jax.sharding import PartitionSpec as P

THETA = 256
MODES = 128
ROWS = 160
LANES = 128
HALF = 64
PARTS = 64
FIVE = 5
CELL = 2 * FIVE


def make_table():
    b, alo, p, k, ahi, s = np.meshgrid(
        np.arange(2), np.arange(2), np.arange(2), np.arange(64), np.arange(2), np.arange(64), indexing="ij"
    )
    angle = 4 * s + 2 * ahi + alo
    wave = 2 * k + b
    phase = ((angle * wave) % THETA).astype(np.float32) * np.float32(2.0 * np.pi / THETA)
    values = np.where(p == 1, -np.sin(phase), np.cos(phase)) * np.float32(THETA ** (-0.5))
    return values.astype(np.float32).reshape(512, 128).astype(jnp.bfloat16)


def low_lanes(shape):
    return lax.broadcasted_iota(jnp.int32, shape, 1) < HALF


def spread_kernel(x_ref, t_ref, o_ref, table_ref, near_ref, scr, sems):
    fetch = [
        pltpu.make_async_copy(x_ref.at[pl.ds(2 * ahi, 2)], near_ref.at[pl.ds(2 * ahi, 2)], sems.at[ahi])
        for ahi in range(2)
    ]
    fetch.append(pltpu.make_async_copy(t_ref, table_ref, sems.at[2]))
    for copy in fetch:
        copy.start()
    low = low_lanes((ROWS, LANES))
    for ahi in range(2):
        fetch[ahi].wait()
        even = near_ref[2 * ahi].astype(jnp.float32)
        odd = near_ref[2 * ahi + 1].astype(jnp.float32)
        scr[pl.ds(ahi, ROWS, stride=2), :] = jnp.where(low, even, pltpu.roll(odd, HALF, 1))
        scr[pl.ds(2 * ROWS + ahi, ROWS, stride=2), :] = jnp.where(low, pltpu.roll(even, HALF, 1), odd)
    o_ref[...] = scr[...].astype(jnp.bfloat16)
    fetch[2].wait()


def transform_kernel(x_ref, t_ref, o_ref, scr_in, scr_out):
    half = lax.axis_index("azim") // (PARTS // 2)
    one = t_ref[pl.ds(pl.multiple_of(256 * half, 256), 256)]
    two = t_ref[pl.ds(pl.multiple_of(256 * (1 - half), 256), 256)]
    scr_in[...] = x_ref[...].astype(jnp.float32)
    low = low_lanes((LANES, LANES))
    def field_of(r5):
        parts = [scr_in[pl.ds(2 * r5 + ahi, PARTS, stride=CELL), :] for ahi in range(2)]
        return jnp.concatenate(parts, axis=0).astype(jnp.bfloat16)

    for base in range(0, FIVE, 2):
        group = range(base, min(base + 2, FIVE))
        field = jnp.concatenate([field_of(r5) for r5 in group], axis=1)
        y = jnp.dot(one, field, preferred_element_type=jnp.float32)
        w = jnp.dot(two, field, preferred_element_type=jnp.float32)
        for i, r5 in enumerate(group):
            at = slice(i * LANES, (i + 1) * LANES)
            straight = jnp.where(low, y[0:128, at], w[128:256, at])
            crossed = jnp.where(low, w[0:128, at], y[128:256, at])
            both = straight + pltpu.roll(crossed, HALF, 1)
            for p in range(2):
                scr_out[pl.ds(2 * r5 + p, PARTS, stride=CELL), :] = both[64 * p : 64 * p + 64]
    o_ref[...] = scr_out[...].astype(jnp.bfloat16)


GAIN = ROWS ** (-0.5)
CHIPS = 4
WIDE = CHIPS * LANES
GRANT = pltpu.CompilerParams(vmem_limit_bytes=16 << 20)


def arrange_kernel(x_ref, o_ref):
    low = low_lanes((2 * ROWS, LANES))
    first = x_ref[0 : 2 * ROWS]
    second = x_ref[2 * ROWS : 4 * ROWS]
    modes = (jnp.where(low, first, second), pltpu.roll(jnp.where(low, second, first), HALF, 1))
    for x in range(CHIPS):
        for m in range(2):
            o_ref[x, m] = modes[m]


def columns_of(left_ref, ref, m, x):
    rows = jnp.concatenate([ref[x, m], ref[x + 1, m]], axis=1)
    g = jnp.dot(left_ref[m], rows, preferred_element_type=jnp.float32) * jnp.float32(GAIN)
    return g[:, :LANES], g[:, LANES:]


def tile_copy(src, dst, m, x, par, sem):
    at = pl.multiple_of((2 * x + par) * LANES, LANES)
    return pltpu.make_async_copy(src.at[x, m], dst.at[m, :, :, pl.ds(at, LANES)], sem)


def both_copy(src, dst, x, par, sem):
    at = pl.multiple_of((2 * x + par) * LANES, LANES)
    return pltpu.make_async_copy(src.at[x], dst.at[:, :, :, pl.ds(at, LANES)], sem)


def store_tile(ref, m, x, value):
    ref[x, m, 0] = value[:LANES]
    ref[x, m, 1] = value[LANES:]


def own_step(mine_ref, xx_ref, xy_ref, left_ref, next_ref, tile, zero, sems, zsems):
    tm = lax.axis_index("tm")
    core = lax.rem(tm, 2)
    zero[...] = jnp.zeros(zero.shape, jnp.float32)

    def blank(dst, j, sem):
        at = pl.multiple_of(j * LANES, LANES)
        return pltpu.make_async_copy(zero, dst.at[:, :, :, pl.ds(at, LANES)], sem)

    def blanks(act):
        @pl.loop(tm + 1, 2 * CHIPS)
        def _(j):
            act(blank(xy_ref, j, zsems.at[0, j]))

        @pl.loop(lax.div(tm + 1, 2), CHIPS)
        def _(x):
            act(blank(xx_ref, 2 * x + 1 - core, zsems.at[1, x]))

    blanks(lambda copy: copy.start())
    even = lax.rem(lax.broadcasted_iota(jnp.int32, (2 * ROWS, LANES), 0), 2) == 0

    @pl.loop(0, 2)
    def _(m):
        f = mine_ref[lax.div(tm, 2), m].astype(jnp.float32)
        turned = jnp.where(even, -pltpu.roll(f, 2 * ROWS - 1, 0), pltpu.roll(f, 1, 0))
        left_ref[m, :LANES] = f.T.astype(jnp.bfloat16)
        left_ref[m, LANES:] = turned.T.astype(jnp.bfloat16)
        for first in range(0, CHIPS, 2):
            for i, block in enumerate(columns_of(left_ref, mine_ref, m, first)):
                x = first + i
                store_tile(tile, m, x, jnp.where(2 * x + core <= tm, block, 0.0))
                tile_copy(tile, xx_ref, m, x, core, sems.at[m, x]).start()
                next_ref[m, x] = pltpu.roll(block, LANES - 1, 1)
        next_ref[m, CHIPS] = jnp.zeros((2 * LANES, LANES), jnp.float32)

    for m in range(2):
        for x in range(CHIPS):
            tile_copy(tile, xx_ref, m, x, core, sems.at[m, x]).wait()
    blanks(lambda copy: copy.wait())


def ahead_kernel(mine_ref, same_ref, *rest):
    del same_ref

    @pl.when(lax.rem(lax.axis_index("tm"), 2) == 1)
    def _():
        own_step(mine_ref, *rest)


def behind_kernel(mine_ref, old_xx, old_xy, old_left, old_next, *rest):
    del old_xx, old_xy, old_left, old_next

    @pl.when(lax.rem(lax.axis_index("tm"), 2) == 0)
    def _():
        own_step(mine_ref, *rest)


def partner_kernel(theirs_ref, left_ref, next_ref, old_xx, old_xy, xx_ref, xy_ref, tile, pair, ynext, sems, ysems):
    del old_xx, old_xy
    tm = lax.axis_index("tm")
    core = lax.rem(tm, 2)
    other = 1 - core
    inner = lax.broadcasted_iota(jnp.int32, (2 * LANES, LANES), 1) < LANES - 1

    ynext[:, CHIPS] = jnp.zeros((2, 2 * LANES, LANES), jnp.float32)
    for first in range(0, CHIPS, 2):

        @pl.when(2 * first + other <= tm + 1)
        def _():
            for m in range(2):
                for i, block in enumerate(columns_of(left_ref, theirs_ref, m, first)):
                    x = first + i
                    store_tile(tile, m, x, block)
                    shifted = pltpu.roll(block, LANES - 1, 1)
                    ynext[m, x] = shifted
                    store_tile(pair.at[1], m, x, jnp.where(inner, shifted, next_ref[m, x + 1 - core]))
            for x in range(first, first + 2):

                @pl.when(2 * x + other <= tm)
                def _():
                    both_copy(tile, xx_ref, x, other, sems.at[x]).start()
                    both_copy(pair.at[1], xy_ref, x, other, ysems.at[1, x]).start()

    for x in range(CHIPS):

        @pl.when(2 * x + core <= tm)
        def _():
            for m in range(2):
                store_tile(pair.at[0], m, x, jnp.where(inner, next_ref[m, x], ynext[m, x + core]))
            both_copy(pair.at[0], xy_ref, x, core, ysems.at[0, x]).start()

    @pl.loop(0, lax.div(tm + 1, 2))
    def _(x):
        both_copy(tile, xx_ref, x, other, sems.at[x]).wait()
        both_copy(pair.at[1], xy_ref, x, other, ysems.at[1, x]).wait()

    @pl.loop(0, lax.div(tm, 2) + 1)
    def _(x):
        both_copy(pair.at[0], xy_ref, x, core, ysems.at[0, x]).wait()


def near(array):
    return pltpu.with_memory_space_constraint(array, pltpu.VMEM)


def kept(array):
    return pltpu.with_memory_space_constraint(array, pltpu.HBM)


def body(pressure):
    f32 = jnp.float32
    bf16 = jnp.bfloat16
    vmem = pl.BlockSpec(memory_space=pltpu.VMEM)
    hbm = pl.BlockSpec(memory_space=pl.ANY)
    far = pl.BlockSpec(memory_space=pltpu.HBM)
    table = jnp.asarray(make_table())
    send, table = pl.pallas_call(
        spread_kernel,
        out_shape=(pltpu.VMEM((640, LANES), bf16), pltpu.VMEM(table.shape, bf16)),
        in_specs=[far, far],
        out_specs=(vmem, vmem),
        scratch_shapes=[
            pltpu.VMEM(pressure.shape, bf16),
            pltpu.VMEM((640, LANES), f32),
            pltpu.SemaphoreType.DMA((3,)),
        ],
        compiler_params=GRANT,
        name="spread",
    )(kept(pressure), kept(table))
    got = lax.all_to_all(send.reshape(PARTS, FIVE, 2, LANES), "azim", 0, 0, tiled=True)
    spectrum = pl.pallas_call(
        transform_kernel,
        out_shape=pltpu.VMEM((640, LANES), bf16),
        in_specs=[vmem, vmem],
        out_specs=vmem,
        scratch_shapes=[pltpu.VMEM((640, LANES), f32), pltpu.VMEM((640, LANES), f32)],
        compiler_params=GRANT,
        name="transform",
    )(near(got.reshape(640, LANES)), near(table))
    owned = lax.all_to_all(spectrum.reshape(PARTS, FIVE, 2, LANES), "azim", 0, 0, tiled=True)
    owned = pl.pallas_call(
        arrange_kernel,
        out_shape=pltpu.VMEM((CHIPS, 2, 2 * ROWS, LANES), bf16),
        in_specs=[vmem],
        out_specs=vmem,
        compiler_params=GRANT,
        name="arrange",
    )(near(owned.reshape(640, LANES)))
    chips = [[2 * x + c for x in range(CHIPS)] for c in range(2)]
    mine = lax.all_to_all(owned, "tm", 0, 0, tiled=True, axis_index_groups=chips)
    out = jax.ShapeDtypeStruct((2, 2, LANES, 2 * WIDE), f32)
    tile = pltpu.VMEM((CHIPS, 2, 2, LANES, LANES), f32)
    steps = (2, CHIPS + 1, 2 * LANES, LANES)
    results = (out, out, pltpu.VMEM((2, 2 * LANES, 2 * ROWS), bf16), pltpu.VMEM(steps, f32))
    scratch = [
        tile,
        pltpu.VMEM((2, 2, LANES, LANES), f32),
        pltpu.SemaphoreType.DMA((2, CHIPS)),
        pltpu.SemaphoreType.DMA((2, 2 * CHIPS)),
    ]
    mine, gram_xx, gram_xy, left, after = pl.pallas_call(
        ahead_kernel,
        out_shape=(pltpu.VMEM(mine.shape, bf16),) + results,
        in_specs=[vmem],
        out_specs=(vmem, hbm, hbm, vmem, vmem),
        scratch_shapes=scratch,
        input_output_aliases={0: 0},
        compiler_params=GRANT,
        name="ahead",
    )(near(mine))
    theirs = lax.ppermute(mine, "tm", [(i, i ^ 1) for i in range(2 * CHIPS)])
    gram_xx, gram_xy, left, after = pl.pallas_call(
        behind_kernel,
        out_shape=results,
        in_specs=[vmem, hbm, hbm, vmem, vmem],
        out_specs=(hbm, hbm, vmem, vmem),
        scratch_shapes=scratch,
        input_output_aliases={1: 0, 2: 1, 3: 2, 4: 3},
        compiler_params=GRANT,
        name="behind",
    )(near(mine), gram_xx, gram_xy, near(left), near(after))
    return pl.pallas_call(
        partner_kernel,
        out_shape=(out, out),
        in_specs=[vmem, vmem, vmem, hbm, hbm],
        out_specs=(hbm, hbm),
        scratch_shapes=[
            tile,
            pltpu.VMEM((2, CHIPS, 2, 2, LANES, LANES), f32),
            pltpu.VMEM(steps, f32),
            pltpu.SemaphoreType.DMA((CHIPS,)),
            pltpu.SemaphoreType.DMA((2, CHIPS)),
        ],
        input_output_aliases={3: 0, 4: 1},
        compiler_params=GRANT,
        name="partner",
    )(near(theirs), near(left), near(after), gram_xx, gram_xy)


def solution(mesh):
    in_specs = (P("azim", None, "tm"),)
    out_specs = (P("azim", None, "tm", None), P("azim", None, "tm", None))
    return jax.shard_map(body, mesh=mesh, in_specs=in_specs, out_specs=out_specs, check_vma=False)
```

```python
import jax
import jax.numpy as jnp
import numpy as np
from jax import lax
from jax.experimental import pallas as pl
from jax.experimental.pallas import tpu as pltpu
from jax.sharding import PartitionSpec as P

THETA = 256
MODES = 128
ROWS = 160
LANES = 128
HALF = 64
PARTS = 64
FIVE = 5
CELL = 2 * FIVE


def make_table():
    b, alo, p, k, ahi, s = np.meshgrid(
        np.arange(2), np.arange(2), np.arange(2), np.arange(64), np.arange(2), np.arange(64), indexing="ij"
    )
    angle = 4 * s + 2 * ahi + alo
    wave = 2 * k + b
    phase = ((angle * wave) % THETA).astype(np.float32) * np.float32(2.0 * np.pi / THETA)
    values = np.where(p == 1, -np.sin(phase), np.cos(phase)) * np.float32(THETA ** (-0.5))
    return values.astype(np.float32).reshape(512, 128).astype(jnp.bfloat16)


def low_lanes(shape):
    return lax.broadcasted_iota(jnp.int32, shape, 1) < HALF


def spread_kernel(x_ref, t_ref, o_ref, table_ref, near_ref, scr, sems):
    fetch = [
        pltpu.make_async_copy(x_ref.at[pl.ds(2 * ahi, 2)], near_ref.at[pl.ds(2 * ahi, 2)], sems.at[ahi])
        for ahi in range(2)
    ]
    fetch.append(pltpu.make_async_copy(t_ref, table_ref, sems.at[2]))
    for copy in fetch:
        copy.start()
    low = low_lanes((ROWS, LANES))
    for ahi in range(2):
        fetch[ahi].wait()
        even = near_ref[2 * ahi].astype(jnp.float32)
        odd = near_ref[2 * ahi + 1].astype(jnp.float32)
        scr[pl.ds(ahi, ROWS, stride=2), :] = jnp.where(low, even, pltpu.roll(odd, HALF, 1))
        scr[pl.ds(2 * ROWS + ahi, ROWS, stride=2), :] = jnp.where(low, pltpu.roll(even, HALF, 1), odd)
    o_ref[...] = scr[...].astype(jnp.bfloat16)
    fetch[2].wait()


def transform_kernel(x_ref, t_ref, o_ref, scr_in, scr_out):
    half = lax.axis_index("azim") // (PARTS // 2)
    one = t_ref[pl.ds(pl.multiple_of(256 * half, 256), 256)]
    two = t_ref[pl.ds(pl.multiple_of(256 * (1 - half), 256), 256)]
    scr_in[...] = x_ref[...].astype(jnp.float32)
    low = low_lanes((LANES, LANES))
    def field_of(r5):
        parts = [scr_in[pl.ds(2 * r5 + ahi, PARTS, stride=CELL), :] for ahi in range(2)]
        return jnp.concatenate(parts, axis=0).astype(jnp.bfloat16)

    for base in range(0, FIVE, 2):
        group = range(base, min(base + 2, FIVE))
        field = jnp.concatenate([field_of(r5) for r5 in group], axis=1)
        y = jnp.dot(one, field, preferred_element_type=jnp.float32)
        w = jnp.dot(two, field, preferred_element_type=jnp.float32)
        for i, r5 in enumerate(group):
            at = slice(i * LANES, (i + 1) * LANES)
            straight = jnp.where(low, y[0:128, at], w[128:256, at])
            crossed = jnp.where(low, w[0:128, at], y[128:256, at])
            both = straight + pltpu.roll(crossed, HALF, 1)
            for p in range(2):
                scr_out[pl.ds(2 * r5 + p, PARTS, stride=CELL), :] = both[64 * p : 64 * p + 64]
    o_ref[...] = scr_out[...].astype(jnp.bfloat16)


GAIN = ROWS ** (-0.5)
CHIPS = 4
WIDE = CHIPS * LANES
GRANT = pltpu.CompilerParams(vmem_limit_bytes=16 << 20)


def columns_of(left_ref, ref, m, x):
    rows = jnp.concatenate([ref[x, m], ref[x + 1, m]], axis=1)
    g = jnp.dot(left_ref[m], rows, preferred_element_type=jnp.float32) * jnp.float32(GAIN)
    return g[:, :LANES], g[:, LANES:]


def tile_copy(src, dst, m, x, par, sem):
    at = pl.multiple_of((2 * x + par) * LANES, LANES)
    return pltpu.make_async_copy(src.at[x, m], dst.at[m, :, :, pl.ds(at, LANES)], sem)


def both_copy(src, dst, x, par, sem):
    at = pl.multiple_of((2 * x + par) * LANES, LANES)
    return pltpu.make_async_copy(src.at[x], dst.at[:, :, :, pl.ds(at, LANES)], sem)


def store_tile(ref, m, x, value):
    ref[x, m, 0] = value[:LANES]
    ref[x, m, 1] = value[LANES:]


def blanks(zero, xx_ref, xy_ref, zsems, act):
    tm = lax.axis_index("tm")
    core = lax.rem(tm, 2)

    def blank(dst, j, sem):
        at = pl.multiple_of(j * LANES, LANES)
        return pltpu.make_async_copy(zero, dst.at[:, :, :, pl.ds(at, LANES)], sem)

    @pl.loop(tm + 1, 2 * CHIPS)
    def _(j):
        act(blank(xy_ref, j, zsems.at[0, j]))

    @pl.loop(lax.div(tm + 1, 2), CHIPS)
    def _(x):
        act(blank(xx_ref, 2 * x + 1 - core, zsems.at[1, x]))


def arrange_kernel(x_ref, o_ref, xx_ref, xy_ref, zero, zsems):
    odd = lax.rem(lax.axis_index("tm"), 2) == 1

    @pl.when(odd)
    def _():
        zero[...] = jnp.zeros(zero.shape, jnp.float32)
        blanks(zero, xx_ref, xy_ref, zsems, lambda copy: copy.start())

    low = low_lanes((2 * ROWS, LANES))
    first = x_ref[0 : 2 * ROWS]
    second = x_ref[2 * ROWS : 4 * ROWS]
    modes = (jnp.where(low, first, second), pltpu.roll(jnp.where(low, second, first), HALF, 1))
    for x in range(CHIPS):
        for m in range(2):
            o_ref[x, m] = modes[m]

    @pl.when(odd)
    def _():
        blanks(zero, xx_ref, xy_ref, zsems, lambda copy: copy.wait())


def own_kernel(mine_ref, old_xx, old_xy, xx_ref, xy_ref, left_ref, next_ref, tile, zero, sems, zsems):
    del old_xx, old_xy
    tm = lax.axis_index("tm")
    core = lax.rem(tm, 2)

    @pl.when(core == 0)
    def _():
        zero[...] = jnp.zeros(zero.shape, jnp.float32)
        blanks(zero, xx_ref, xy_ref, zsems, lambda copy: copy.start())

    even = lax.rem(lax.broadcasted_iota(jnp.int32, (2 * ROWS, LANES), 0), 2) == 0

    @pl.loop(0, 2)
    def _(m):
        f = mine_ref[lax.div(tm, 2), m].astype(jnp.float32)
        turned = jnp.where(even, -pltpu.roll(f, 2 * ROWS - 1, 0), pltpu.roll(f, 1, 0))
        left_ref[m, :LANES] = f.T.astype(jnp.bfloat16)
        left_ref[m, LANES:] = turned.T.astype(jnp.bfloat16)
        for first in range(0, CHIPS, 2):
            for i, block in enumerate(columns_of(left_ref, mine_ref, m, first)):
                x = first + i
                store_tile(tile, m, x, jnp.where(2 * x + core <= tm, block, 0.0))
                tile_copy(tile, xx_ref, m, x, core, sems.at[m, x]).start()
                next_ref[m, x] = pltpu.roll(block, LANES - 1, 1)
        next_ref[m, CHIPS] = jnp.zeros((2 * LANES, LANES), jnp.float32)

    for m in range(2):
        for x in range(CHIPS):
            tile_copy(tile, xx_ref, m, x, core, sems.at[m, x]).wait()

    @pl.when(core == 0)
    def _():
        blanks(zero, xx_ref, xy_ref, zsems, lambda copy: copy.wait())


def partner_kernel(theirs_ref, left_ref, next_ref, old_xx, old_xy, xx_ref, xy_ref, tile, pair, ynext, sems, ysems):
    del old_xx, old_xy
    tm = lax.axis_index("tm")
    core = lax.rem(tm, 2)
    other = 1 - core
    inner = lax.broadcasted_iota(jnp.int32, (2 * LANES, LANES), 1) < LANES - 1

    ynext[:, CHIPS] = jnp.zeros((2, 2 * LANES, LANES), jnp.float32)
    for first in range(0, CHIPS, 2):

        @pl.when(2 * first + other <= tm + 1)
        def _():
            for m in range(2):
                for i, block in enumerate(columns_of(left_ref, theirs_ref, m, first)):
                    x = first + i
                    store_tile(tile, m, x, block)
                    shifted = pltpu.roll(block, LANES - 1, 1)
                    ynext[m, x] = shifted
                    store_tile(pair.at[1], m, x, jnp.where(inner, shifted, next_ref[m, x + 1 - core]))
            for x in range(first, first + 2):

                @pl.when(2 * x + other <= tm)
                def _():
                    both_copy(tile, xx_ref, x, other, sems.at[x]).start()
                    both_copy(pair.at[1], xy_ref, x, other, ysems.at[1, x]).start()

    for x in range(CHIPS):

        @pl.when(2 * x + core <= tm)
        def _():
            for m in range(2):
                store_tile(pair.at[0], m, x, jnp.where(inner, next_ref[m, x], ynext[m, x + core]))
            both_copy(pair.at[0], xy_ref, x, core, ysems.at[0, x]).start()

    @pl.loop(0, lax.div(tm + 1, 2))
    def _(x):
        both_copy(tile, xx_ref, x, other, sems.at[x]).wait()
        both_copy(pair.at[1], xy_ref, x, other, ysems.at[1, x]).wait()

    @pl.loop(0, lax.div(tm, 2) + 1)
    def _(x):
        both_copy(pair.at[0], xy_ref, x, core, ysems.at[0, x]).wait()


def near(array):
    return pltpu.with_memory_space_constraint(array, pltpu.VMEM)


def kept(array):
    return pltpu.with_memory_space_constraint(array, pltpu.HBM)


def body(pressure):
    f32 = jnp.float32
    bf16 = jnp.bfloat16
    vmem = pl.BlockSpec(memory_space=pltpu.VMEM)
    hbm = pl.BlockSpec(memory_space=pl.ANY)
    far = pl.BlockSpec(memory_space=pltpu.HBM)
    table = jnp.asarray(make_table())
    send, table = pl.pallas_call(
        spread_kernel,
        out_shape=(pltpu.VMEM((640, LANES), bf16), pltpu.VMEM(table.shape, bf16)),
        in_specs=[far, far],
        out_specs=(vmem, vmem),
        scratch_shapes=[
            pltpu.VMEM(pressure.shape, bf16),
            pltpu.VMEM((640, LANES), f32),
            pltpu.SemaphoreType.DMA((3,)),
        ],
        compiler_params=GRANT,
        name="spread",
    )(kept(pressure), kept(table))
    got = lax.all_to_all(send.reshape(PARTS, FIVE, 2, LANES), "azim", 0, 0, tiled=True)
    spectrum = pl.pallas_call(
        transform_kernel,
        out_shape=pltpu.VMEM((640, LANES), bf16),
        in_specs=[vmem, vmem],
        out_specs=vmem,
        scratch_shapes=[pltpu.VMEM((640, LANES), f32), pltpu.VMEM((640, LANES), f32)],
        compiler_params=GRANT,
        name="transform",
    )(near(got.reshape(640, LANES)), near(table))
    owned = lax.all_to_all(spectrum.reshape(PARTS, FIVE, 2, LANES), "azim", 0, 0, tiled=True)
    out = jax.ShapeDtypeStruct((2, 2, LANES, 2 * WIDE), f32)
    blank = [pltpu.VMEM((2, 2, LANES, LANES), f32), pltpu.SemaphoreType.DMA((2, 2 * CHIPS))]
    owned, gram_xx, gram_xy = pl.pallas_call(
        arrange_kernel,
        out_shape=(pltpu.VMEM((CHIPS, 2, 2 * ROWS, LANES), bf16), out, out),
        in_specs=[vmem],
        out_specs=(vmem, hbm, hbm),
        scratch_shapes=blank,
        compiler_params=GRANT,
        name="arrange",
    )(near(owned.reshape(640, LANES)))
    chips = [[2 * x + c for x in range(CHIPS)] for c in range(2)]
    mine = lax.all_to_all(owned, "tm", 0, 0, tiled=True, axis_index_groups=chips)
    theirs = lax.ppermute(mine, "tm", [(i, i ^ 1) for i in range(2 * CHIPS)])
    tile = pltpu.VMEM((CHIPS, 2, 2, LANES, LANES), f32)
    steps = (2, CHIPS + 1, 2 * LANES, LANES)
    gram_xx, gram_xy, left, after = pl.pallas_call(
        own_kernel,
        out_shape=(out, out, pltpu.VMEM((2, 2 * LANES, 2 * ROWS), bf16), pltpu.VMEM(steps, f32)),
        in_specs=[vmem, hbm, hbm],
        out_specs=(hbm, hbm, vmem, vmem),
        scratch_shapes=[tile, blank[0], pltpu.SemaphoreType.DMA((2, CHIPS)), blank[1]],
        input_output_aliases={1: 0, 2: 1},
        compiler_params=GRANT,
        name="own",
    )(near(mine), gram_xx, gram_xy)
    return pl.pallas_call(
        partner_kernel,
        out_shape=(out, out),
        in_specs=[vmem, vmem, vmem, hbm, hbm],
        out_specs=(hbm, hbm),
        scratch_shapes=[
            tile,
            pltpu.VMEM((2, CHIPS, 2, 2, LANES, LANES), f32),
            pltpu.VMEM(steps, f32),
            pltpu.SemaphoreType.DMA((CHIPS,)),
            pltpu.SemaphoreType.DMA((2, CHIPS)),
        ],
        input_output_aliases={3: 0, 4: 1},
        compiler_params=GRANT,
        name="partner",
    )(near(theirs), near(left), near(after), gram_xx, gram_xy)


def solution(mesh):
    in_specs = (P("azim", None, "tm"),)
    out_specs = (P("azim", None, "tm", None), P("azim", None, "tm", None))
    return jax.shard_map(body, mesh=mesh, in_specs=in_specs, out_specs=out_specs, check_vma=False)
```

```python
import jax
import jax.numpy as jnp
import numpy as np
from jax import lax
from jax.experimental import pallas as pl
from jax.experimental.pallas import tpu as pltpu
from jax.sharding import PartitionSpec as P

THETA = 256
MODES = 128
ROWS = 160
LANES = 128
HALF = 64
PARTS = 64
FIVE = 5
CELL = 2 * FIVE


def make_table():
    b, alo, p, k, ahi, s = np.meshgrid(
        np.arange(2), np.arange(2), np.arange(2), np.arange(64), np.arange(2), np.arange(64), indexing="ij"
    )
    angle = 4 * s + 2 * ahi + alo
    wave = 2 * k + b
    phase = ((angle * wave) % THETA).astype(np.float32) * np.float32(2.0 * np.pi / THETA)
    values = np.where(p == 1, -np.sin(phase), np.cos(phase)) * np.float32(THETA ** (-0.5))
    return values.astype(np.float32).reshape(512, 128).astype(jnp.bfloat16)


def low_lanes(shape):
    return lax.broadcasted_iota(jnp.int32, shape, 1) < HALF


def spread_kernel(x_ref, t_ref, o_ref, table_ref, near_ref, scr, sems):
    fetch = [
        pltpu.make_async_copy(x_ref.at[pl.ds(2 * ahi, 2)], near_ref.at[pl.ds(2 * ahi, 2)], sems.at[ahi])
        for ahi in range(2)
    ]
    fetch.append(pltpu.make_async_copy(t_ref, table_ref, sems.at[2]))
    for copy in fetch:
        copy.start()
    low = low_lanes((ROWS, LANES))
    for ahi in range(2):
        fetch[ahi].wait()
        even = near_ref[2 * ahi].astype(jnp.float32)
        odd = near_ref[2 * ahi + 1].astype(jnp.float32)
        scr[pl.ds(ahi, ROWS, stride=2), :] = jnp.where(low, even, pltpu.roll(odd, HALF, 1))
        scr[pl.ds(2 * ROWS + ahi, ROWS, stride=2), :] = jnp.where(low, pltpu.roll(even, HALF, 1), odd)
    o_ref[...] = scr[...].astype(jnp.bfloat16)
    fetch[2].wait()


def transform_kernel(x_ref, t_ref, o_ref, scr_in, scr_out):
    half = lax.axis_index("azim") // (PARTS // 2)
    one = t_ref[pl.ds(pl.multiple_of(256 * half, 256), 256)]
    two = t_ref[pl.ds(pl.multiple_of(256 * (1 - half), 256), 256)]
    scr_in[...] = x_ref[...].astype(jnp.float32)
    low = low_lanes((LANES, LANES))
    for r5 in range(FIVE):
        field = jnp.concatenate(
            [scr_in[pl.ds(2 * r5 + ahi, PARTS, stride=CELL), :] for ahi in range(2)], axis=0
        ).astype(jnp.bfloat16)
        y = jnp.dot(one, field, preferred_element_type=jnp.float32)
        w = jnp.dot(two, field, preferred_element_type=jnp.float32)
        straight = jnp.where(low, y[0:128], w[128:256])
        crossed = jnp.where(low, w[0:128], y[128:256])
        both = straight + pltpu.roll(crossed, HALF, 1)
        for p in range(2):
            scr_out[pl.ds(2 * r5 + p, PARTS, stride=CELL), :] = both[64 * p : 64 * p + 64]
    o_ref[...] = scr_out[...].astype(jnp.bfloat16)


GAIN = ROWS ** (-0.5)
CHIPS = 4
WIDE = CHIPS * LANES
GRANT = pltpu.CompilerParams(vmem_limit_bytes=16 << 20)


def arrange_kernel(x_ref, o_ref):
    low = low_lanes((2 * ROWS, LANES))
    first = x_ref[0 : 2 * ROWS]
    second = x_ref[2 * ROWS : 4 * ROWS]
    modes = (jnp.where(low, first, second), pltpu.roll(jnp.where(low, second, first), HALF, 1))
    for x in range(CHIPS):
        for m in range(2):
            o_ref[x, m] = modes[m]


def columns_of(left_ref, ref, m, x):
    rows = jnp.concatenate([ref[x, m], ref[x + 1, m]], axis=1)
    g = jnp.dot(left_ref[m], rows, preferred_element_type=jnp.float32) * jnp.float32(GAIN)
    return g[:, :LANES], g[:, LANES:]


def tile_copy(src, dst, m, x, par, sem):
    at = pl.multiple_of((2 * x + par) * LANES, LANES)
    return pltpu.make_async_copy(src.at[x, m], dst.at[m, :, :, pl.ds(at, LANES)], sem)


def both_copy(src, dst, x, par, sem):
    at = pl.multiple_of((2 * x + par) * LANES, LANES)
    return pltpu.make_async_copy(src.at[x], dst.at[:, :, :, pl.ds(at, LANES)], sem)


def store_tile(ref, m, x, value):
    ref[x, m, 0] = value[:LANES]
    ref[x, m, 1] = value[LANES:]


def own_step(mine_ref, xx_ref, xy_ref, left_ref, next_ref, tile, zero, sems, zsems):
    tm = lax.axis_index("tm")
    core = lax.rem(tm, 2)
    zero[...] = jnp.zeros(zero.shape, jnp.float32)

    def blank(dst, j, sem):
        at = pl.multiple_of(j * LANES, LANES)
        return pltpu.make_async_copy(zero, dst.at[:, :, :, pl.ds(at, LANES)], sem)

    def blanks(act):
        @pl.loop(tm + 1, 2 * CHIPS)
        def _(j):
            act(blank(xy_ref, j, zsems.at[0, j]))

        @pl.loop(lax.div(tm + 1, 2), CHIPS)
        def _(x):
            act(blank(xx_ref, 2 * x + 1 - core, zsems.at[1, x]))

    blanks(lambda copy: copy.start())
    even = lax.rem(lax.broadcasted_iota(jnp.int32, (2 * ROWS, LANES), 0), 2) == 0

    @pl.loop(0, 2)
    def _(m):
        f = mine_ref[lax.div(tm, 2), m].astype(jnp.float32)
        turned = jnp.where(even, -pltpu.roll(f, 2 * ROWS - 1, 0), pltpu.roll(f, 1, 0))
        left_ref[m, :LANES] = f.T.astype(jnp.bfloat16)
        left_ref[m, LANES:] = turned.T.astype(jnp.bfloat16)
        for first in range(0, CHIPS, 2):
            for i, block in enumerate(columns_of(left_ref, mine_ref, m, first)):
                x = first + i
                store_tile(tile, m, x, jnp.where(2 * x + core <= tm, block, 0.0))
                tile_copy(tile, xx_ref, m, x, core, sems.at[m, x]).start()
                next_ref[m, x] = pltpu.roll(block, LANES - 1, 1)
        next_ref[m, CHIPS] = jnp.zeros((2 * LANES, LANES), jnp.float32)

    for m in range(2):
        for x in range(CHIPS):
            tile_copy(tile, xx_ref, m, x, core, sems.at[m, x]).wait()
    blanks(lambda copy: copy.wait())


def ahead_kernel(mine_ref, same_ref, *rest):
    del same_ref

    @pl.when(lax.rem(lax.axis_index("tm"), 2) == 1)
    def _():
        own_step(mine_ref, *rest)


def behind_kernel(mine_ref, old_xx, old_xy, old_left, old_next, *rest):
    del old_xx, old_xy, old_left, old_next

    @pl.when(lax.rem(lax.axis_index("tm"), 2) == 0)
    def _():
        own_step(mine_ref, *rest)


def partner_kernel(theirs_ref, left_ref, next_ref, old_xx, old_xy, xx_ref, xy_ref, tile, pair, ynext, sems, ysems):
    del old_xx, old_xy
    tm = lax.axis_index("tm")
    core = lax.rem(tm, 2)
    other = 1 - core
    inner = lax.broadcasted_iota(jnp.int32, (2 * LANES, LANES), 1) < LANES - 1

    ynext[:, CHIPS] = jnp.zeros((2, 2 * LANES, LANES), jnp.float32)
    for first in range(0, CHIPS, 2):

        @pl.when(2 * first + other <= tm + 1)
        def _():
            for m in range(2):
                for i, block in enumerate(columns_of(left_ref, theirs_ref, m, first)):
                    x = first + i
                    store_tile(tile, m, x, block)
                    shifted = pltpu.roll(block, LANES - 1, 1)
                    ynext[m, x] = shifted
                    store_tile(pair.at[1], m, x, jnp.where(inner, shifted, next_ref[m, x + 1 - core]))
            for x in range(first, first + 2):

                @pl.when(2 * x + other <= tm)
                def _():
                    both_copy(tile, xx_ref, x, other, sems.at[x]).start()
                    both_copy(pair.at[1], xy_ref, x, other, ysems.at[1, x]).start()

    for x in range(CHIPS):

        @pl.when(2 * x + core <= tm)
        def _():
            for m in range(2):
                store_tile(pair.at[0], m, x, jnp.where(inner, next_ref[m, x], ynext[m, x + core]))
            both_copy(pair.at[0], xy_ref, x, core, ysems.at[0, x]).start()

    @pl.loop(0, lax.div(tm + 1, 2))
    def _(x):
        both_copy(tile, xx_ref, x, other, sems.at[x]).wait()
        both_copy(pair.at[1], xy_ref, x, other, ysems.at[1, x]).wait()

    @pl.loop(0, lax.div(tm, 2) + 1)
    def _(x):
        both_copy(pair.at[0], xy_ref, x, core, ysems.at[0, x]).wait()


def near(array):
    return pltpu.with_memory_space_constraint(array, pltpu.VMEM)


def kept(array):
    return pltpu.with_memory_space_constraint(array, pltpu.HBM)


def body(pressure):
    f32 = jnp.float32
    bf16 = jnp.bfloat16
    vmem = pl.BlockSpec(memory_space=pltpu.VMEM)
    hbm = pl.BlockSpec(memory_space=pl.ANY)
    far = pl.BlockSpec(memory_space=pltpu.HBM)
    table = jnp.asarray(make_table())
    send, table = pl.pallas_call(
        spread_kernel,
        out_shape=(pltpu.VMEM((640, LANES), bf16), pltpu.VMEM(table.shape, bf16)),
        in_specs=[far, far],
        out_specs=(vmem, vmem),
        scratch_shapes=[
            pltpu.VMEM(pressure.shape, bf16),
            pltpu.VMEM((640, LANES), f32),
            pltpu.SemaphoreType.DMA((3,)),
        ],
        compiler_params=GRANT,
        name="spread",
    )(kept(pressure), kept(table))
    got = lax.all_to_all(send.reshape(PARTS, FIVE, 2, LANES), "azim", 0, 0, tiled=True)
    spectrum = pl.pallas_call(
        transform_kernel,
        out_shape=pltpu.VMEM((640, LANES), bf16),
        in_specs=[vmem, vmem],
        out_specs=vmem,
        scratch_shapes=[pltpu.VMEM((640, LANES), f32), pltpu.VMEM((640, LANES), f32)],
        compiler_params=GRANT,
        name="transform",
    )(near(got.reshape(640, LANES)), near(table))
    owned = lax.all_to_all(spectrum.reshape(PARTS, FIVE, 2, LANES), "azim", 0, 0, tiled=True)
    owned = pl.pallas_call(
        arrange_kernel,
        out_shape=pltpu.VMEM((CHIPS, 2, 2 * ROWS, LANES), bf16),
        in_specs=[vmem],
        out_specs=vmem,
        compiler_params=GRANT,
        name="arrange",
    )(near(owned.reshape(640, LANES)))
    chips = [[2 * x + c for x in range(CHIPS)] for c in range(2)]
    mine = lax.all_to_all(owned, "tm", 0, 0, tiled=True, axis_index_groups=chips)
    out = jax.ShapeDtypeStruct((2, 2, LANES, 2 * WIDE), f32)
    tile = pltpu.VMEM((CHIPS, 2, 2, LANES, LANES), f32)
    steps = (2, CHIPS + 1, 2 * LANES, LANES)
    results = (out, out, pltpu.VMEM((2, 2 * LANES, 2 * ROWS), bf16), pltpu.VMEM(steps, f32))
    scratch = [
        tile,
        pltpu.VMEM((2, 2, LANES, LANES), f32),
        pltpu.SemaphoreType.DMA((2, CHIPS)),
        pltpu.SemaphoreType.DMA((2, 2 * CHIPS)),
    ]
    mine, gram_xx, gram_xy, left, after = pl.pallas_call(
        ahead_kernel,
        out_shape=(pltpu.VMEM(mine.shape, bf16),) + results,
        in_specs=[vmem],
        out_specs=(vmem, hbm, hbm, vmem, vmem),
        scratch_shapes=scratch,
        input_output_aliases={0: 0},
        compiler_params=GRANT,
        name="ahead",
    )(near(mine))
    theirs = lax.ppermute(mine, "tm", [(i, i ^ 1) for i in range(2 * CHIPS)])
    gram_xx, gram_xy, left, after = pl.pallas_call(
        behind_kernel,
        out_shape=results,
        in_specs=[vmem, hbm, hbm, vmem, vmem],
        out_specs=(hbm, hbm, vmem, vmem),
        scratch_shapes=scratch,
        input_output_aliases={1: 0, 2: 1, 3: 2, 4: 3},
        compiler_params=GRANT,
        name="behind",
    )(near(mine), gram_xx, gram_xy, near(left), near(after))
    return pl.pallas_call(
        partner_kernel,
        out_shape=(out, out),
        in_specs=[vmem, vmem, vmem, hbm, hbm],
        out_specs=(hbm, hbm),
        scratch_shapes=[
            tile,
            pltpu.VMEM((2, CHIPS, 2, 2, LANES, LANES), f32),
            pltpu.VMEM(steps, f32),
            pltpu.SemaphoreType.DMA((CHIPS,)),
            pltpu.SemaphoreType.DMA((2, CHIPS)),
        ],
        input_output_aliases={3: 0, 4: 1},
        compiler_params=GRANT,
        name="partner",
    )(near(theirs), near(left), near(after), gram_xx, gram_xy)


def solution(mesh):
    in_specs = (P("azim", None, "tm"),)
    out_specs = (P("azim", None, "tm", None), P("azim", None, "tm", None))
    return jax.shard_map(body, mesh=mesh, in_specs=in_specs, out_specs=out_specs, check_vma=False)
```
